32 devices in a mesh: rep: 4 (over y, x), row: 8 (over z, core).
Axes of the slice: x: 2, y: 2, z: 4, core: 2. Of those that a mesh axis runs over, the one named last changes fastest.
Arguments:
- node_feat: float32 [4096, 256], P(('rep', 'row')), may hold values from -6 to 6
- weight: float32 [256, 256], replicated, may hold values from -0.375 to 0.375
- bias: float32 [256], replicated, may hold values from -0.5 to 0.5
- cotangent: float32 [4096, 256], P(('rep', 'row')), may hold values from -6 to 6
- blocks: float32 [4, 8, 64, 4096], P('rep', 'row'), may hold values from -0.1875 to 0.1875
- row_block: int32 [4, 8, 64], P('rep', 'row'), may hold values from 0 to 7
- col_block: int32 [4, 8, 64], P('rep', 'row'), may hold values from 0 to 3
- live_blocks: int32 [4, 8], P('rep', 'row'), may hold values from 12 to 64, as said below
- send_list: int32 [4, 2048], P('rep'), may hold values from 0 to 127
Outputs:
- activated: float32 [4096, 256], P(('rep', 'row'))
- feat_grad: float32 [4096, 256], P(('rep', 'row'))
- weight_grad: float32 [256, 256], replicated
- bias_grad: float32 [256], replicated
The draws below stay inside these ranges and needn't reach their ends.
Inputs may be any that keep to these rules, and one draw needn't show every extreme that they name: `live_blocks`: each value is 64 divided by a whole number from 1 to 5, rounded down; some device has all 64 slots used.
All inputs are finite; a program needn't handle non-finite values.
Results may differ from the reference program's by a relative error of at most 0.0001.
Values sent between devices are 32-bit elements; how exact they have to be, the bound alone decides.
No kernel may reach another device: no remote copies, remote signals or barrier semaphores. Data moves between devices by JAX's collectives and lax.ppermute only.
A program may use at most 64 MiB of HBM per device.

```python
import jax
import jax.numpy as jnp
from jax import lax

F = 256
NODE_DEV = 128
BS = 64
BND = 32
CAP = 64
RGB = 8
NCOLB = 4
NODES = 4096
N_REP = 4
N_ROW = 8


def draw_live_blocks(key, part):
    divisor = jax.random.randint(key, (N_REP * N_ROW,), 1, 6)
    counts = (CAP // divisor).astype(jnp.int32)
    place = jax.random.randint(jax.random.fold_in(key, 7), (), 0, N_REP * N_ROW)
    counts = counts.at[place].set(CAP)
    return counts.reshape(N_REP, N_ROW).astype(jnp.int32)


def place_ends(array, key, least, largest):
    extent = array.shape
    spot = [jax.random.randint(jax.random.fold_in(key, axis), (), 0, extent[axis]) for axis in range(len(extent))]
    array = array.at[tuple(spot)].set(least)
    longest = extent.index(max(extent))
    spot[longest] = (spot[longest] + 1) % extent[longest]
    return array.at[tuple(spot)].set(largest)


def block_levels(key, extent, cuts, least, largest):
    def one(dim, shards_of):
        heights = jax.random.uniform(jax.random.fold_in(jax.random.fold_in(key, 6), dim), (shards_of,), jnp.float32, least / len(cuts), largest / len(cuts))
        return jnp.repeat(jnp.exp(heights), extent[dim] // shards_of).reshape((-1,) + (1,) * (len(extent) - dim - 1))

    gain = one(*cuts[0])
    for cut in cuts[1:]:
        gain = gain * one(*cut)
    return gain


def normal_values(stream_key, shape, deviation, limit, cuts=(), kind=jnp.bfloat16):
    values = jax.random.normal(stream_key, shape, jnp.float32) * deviation
    if len(cuts) > 0:
        values = block_levels(stream_key, shape, cuts, -0.22, 0.18) * values
    return jnp.clip(values, min=-limit, max=limit).astype(kind)


def setup_inputs(seed: int = 0) -> dict:
    streams_of = jax.random.split(jax.random.key(seed), 10)
    return {
        "node_feat": normal_values(streams_of[0], (NODES, F), 1.0, 6.0, ((0, 32),), jnp.float32),
        "weight": normal_values(streams_of[1], (F, F), F ** -0.5, 0.375, (), jnp.float32),
        "bias": jnp.clip(jax.random.uniform(streams_of[2], (F,), jnp.float32, -0.5, 0.5), -0.5, 0.5),
        "cotangent": normal_values(streams_of[3], (NODES, F), 1.0, 6.0, ((0, 32),), jnp.float32),
        "blocks": normal_values(streams_of[4], (N_REP, N_ROW, CAP, BS * BS), (CAP * BS * BS // (2 * NODE_DEV)) ** -0.5, 0.1875, ((0, 4), (1, 8)), jnp.float32),
        "row_block": place_ends(jax.random.randint(streams_of[5], (N_REP, N_ROW, CAP), 0, RGB), jax.random.fold_in(streams_of[5], 1), 0, RGB - 1).astype(jnp.int32),
        "col_block": place_ends(jax.random.randint(streams_of[6], (N_REP, N_ROW, CAP), 0, NCOLB), jax.random.fold_in(streams_of[6], 1), 0, NCOLB - 1).astype(jnp.int32),
        "live_blocks": draw_live_blocks(jax.random.fold_in(streams_of[9], 71), 0),
        "send_list": place_ends(jax.random.randint(streams_of[8], (N_REP, N_ROW * N_ROW * BND), 0, NODE_DEV), jax.random.fold_in(streams_of[8], 1), 0, NODE_DEV - 1).astype(jnp.int32),
    }


def reference(node_feat, weight, bias, cotangent, blocks, row_block, col_block, live_blocks, send_list):
    highest = lax.Precision.HIGHEST
    projected = jnp.dot(node_feat, weight, precision=highest, preferred_element_type=jnp.float32)
    shard_proj = projected.reshape(N_REP, N_ROW, NODE_DEV, F)
    live_mask = (jnp.arange(CAP)[None, None, :] < live_blocks[:, :, None]).astype(jnp.float32)
    masked = blocks.reshape(N_REP, N_ROW, CAP, BS, BS) * live_mask[:, :, :, None, None]
    lists = send_list.reshape(N_REP, N_ROW, N_ROW, BND)
    member_ids = jnp.arange(N_ROW)

    def forward_group(carry, group):
        group_proj = shard_proj[group]

        def forward_member(member):
            wanted_rows = lists[group][:, member, :]
            border_rows = jnp.take_along_axis(group_proj, wanted_rows[:, :, None], axis=1)
            columns = border_rows.reshape(NCOLB, BS, F)[col_block[group, member]]
            product = jnp.einsum("kij,kjf->kif", masked[group, member], columns, precision=highest)
            return jax.ops.segment_sum(product, row_block[group, member], num_segments=RGB).reshape(N_REP, NODE_DEV, F)

        pieces = lax.map(forward_member, member_ids)
        return carry + jnp.swapaxes(pieces, 0, 1), None

    zero_acc = jnp.zeros((N_REP, N_ROW, NODE_DEV, F), jnp.float32)
    summed, unused_out = lax.scan(forward_group, zero_acc, jnp.arange(N_REP))
    pre_act = summed.reshape(NODES, F) + bias[None, :]
    sigmoid_pre = jax.nn.sigmoid(pre_act)
    activated = pre_act * sigmoid_pre
    grad_pre = cotangent * (sigmoid_pre * (1.0 + pre_act * (1.0 - sigmoid_pre)))
    grad_shards = grad_pre.reshape(N_REP, N_ROW, NODE_DEV, F)

    def backward_group(group):
        def backward_member(member):
            group_grad = grad_shards[:, member].reshape(RGB, BS, F)
            contribution = jnp.einsum("kij,kif->kjf", masked[group, member], group_grad[row_block[group, member]], precision=highest)
            return jax.ops.segment_sum(contribution, col_block[group, member], num_segments=NCOLB).reshape(N_ROW, BND, F)

        border_grad = lax.map(backward_member, member_ids)

        def collect_owner(owner):
            terms = border_grad[:, owner].reshape(N_ROW * BND, F)
            targets = lists[group][owner].reshape(N_ROW * BND)
            return jax.ops.segment_sum(terms, targets, num_segments=NODE_DEV)

        return lax.map(collect_owner, member_ids)

    proj_grad = lax.map(backward_group, jnp.arange(N_REP)).reshape(NODES, F)
    feat_grad = jnp.dot(proj_grad, weight.T, precision=highest, preferred_element_type=jnp.float32)
    weight_grad = jnp.dot(node_feat.T, proj_grad, precision=highest, preferred_element_type=jnp.float32)
    bias_grad = jnp.sum(grad_pre, axis=0)
    return (activated, feat_grad, weight_grad, bias_grad)
```

```python
import functools

import jax
import jax.numpy as jnp
from jax import lax
from jax.experimental import pallas as pl
from jax.experimental.pallas import tpu as pltpu
from jax.sharding import PartitionSpec as P

BS = 64
LANES = 128
PAD = 8
F32 = jnp.float32
BF16 = jnp.bfloat16
NN = (((1,), (0,)), ((), ()))
TN = (((0,), (0,)), ((), ()))
NT = (((1,), (1,)), ((), ()))


def split(x):
    high = x.astype(BF16)
    return high, (x - high.astype(F32)).astype(BF16)


def mm(a, b, dims):
    return lax.dot_general(a, b, dims, preferred_element_type=F32)


def mm3(a, b, dims):
    return mm(a[0], b[0], dims) + (mm(a[0], b[1], dims) + mm(a[1], b[0], dims))


def call(kernel, outs, args, scratch=(), flops=0, smem=()):
    out_bytes = sum(int(o.size) * o.dtype.itemsize for o in outs)
    in_bytes = sum(int(a.size) * a.dtype.itemsize for a in args)
    return pl.pallas_call(
        kernel,
        out_shape=outs,
        in_specs=[
            pl.BlockSpec(memory_space=pltpu.SMEM if k in smem else pltpu.VMEM)
            for k in range(len(args))
        ],
        out_specs=[pl.BlockSpec(memory_space=pltpu.VMEM) for _ in outs],
        scratch_shapes=list(scratch),
        cost_estimate=pl.CostEstimate(
            flops=flops, transcendentals=0, bytes_accessed=in_bytes + out_bytes
        ),
        name=kernel.func.__name__ if hasattr(kernel, "func") else kernel.__name__,
    )(*args)


def rows_at(index, count):
    return pl.ds(pl.multiple_of(index * count, count), count)


def one_hot(list_ref, me, slots, nodes):
    wanted = list_ref[:, rows_at(me, slots)]
    node = lax.broadcasted_iota(jnp.int32, (nodes, slots), 0)
    return (node == wanted).astype(BF16)


def gather_rows(members, list_ref, feat_ref, *refs):
    outs, buffer = refs[:-1], refs[-1]
    me = lax.axis_index("row")
    nodes = feat_ref.shape[0]
    slots = buffer.shape[0]
    pick = one_hot(list_ref, me, slots, nodes)
    high, low = split(feat_ref[...])
    buffer[...] = mm(pick, high, TN) + mm(pick, low, TN)
    for s in range(members):
        outs[s][...] = buffer[rows_at(lax.bitwise_xor(me, s), slots // members), :]


def aggregate(me_count, groups, row_blocks, dense_ref, *refs):
    pieces, outs = refs[:me_count], refs[me_count : me_count + groups]
    border, natural = refs[me_count + groups :]
    me, group = lax.axis_index("row"), lax.axis_index("rep")
    per = pieces[0].shape[0]
    for s in range(me_count):
        border[rows_at(lax.bitwise_xor(me, s), per), :] = pieces[s][...]
    result = mm3(split(dense_ref[...]), split(border[...]), NN)
    unmix(result, natural, row_blocks)
    nodes = outs[0].shape[0]
    for s in range(groups):
        for part in range(natural.shape[0]):
            outs[s][:, part * LANES : (part + 1) * LANES] = natural[
                part, rows_at(lax.bitwise_xor(group, s), nodes), :
            ]


def unmix(result, natural, row_blocks):
    for m in range(BS):
        start = ((m % 2) * (BS // 2) + m // 2) * row_blocks
        for part in range(natural.shape[0]):
            natural[part, pl.ds(m, row_blocks, stride=BS), :] = result[
                start : start + row_blocks, part * LANES : (part + 1) * LANES
            ]


def activate(groups, members, *refs):
    pieces = refs[:groups]
    weight_ref, bias_ref, cot_ref, act_ref, grad_ref, keep_ref, send_ref, part_ref, buffer = refs[groups:]
    me = lax.axis_index("row")
    total = pieces[0][...]
    for s in range(1, groups):
        total = total + pieces[s][...]
    total_split = split(total)
    pre = mm3(total_split, split(weight_ref[...]), NN) + bias_ref[...]
    gate = jax.nn.sigmoid(pre)
    act_ref[...] = pre * gate
    grad = cot_ref[...] * (gate * (1.0 + pre * (1.0 - gate)))
    grad_ref[...] = grad
    buffer[...] = mm3(total_split, split(grad), TN)
    half = members // 2
    chunk = buffer.shape[0] // members
    bits = members.bit_length() - 1
    for k in range(members):
        s = int(format(k, f"0{bits}b")[::-1], 2)
        value = buffer[rows_at(lax.bitwise_xor(me, s), chunk), :]
        target = keep_ref if k < half else send_ref
        k = k % half
        target[k * chunk : (k + 1) * chunk, :] = value
    sums = jnp.sum(grad, axis=0, keepdims=True)
    part_ref[...] = jnp.broadcast_to(sums, part_ref.shape)


def spread(groups, members, row_blocks, dense_ref, *refs):
    pieces, outs = refs[:groups], refs[groups : groups + members]
    natural, border = refs[groups + members :]
    me, group = lax.axis_index("row"), lax.axis_index("rep")
    nodes = pieces[0].shape[0]
    for s in range(groups):
        for part in range(natural.shape[0]):
            natural[part, rows_at(lax.bitwise_xor(group, s), nodes), :] = pieces[s][
                :, part * LANES : (part + 1) * LANES
            ]
    order = []
    for parity in range(2):
        for t in range(BS // 2):
            order.append(
                jnp.concatenate(
                    [
                        natural[part, pl.ds(2 * t + parity, row_blocks, stride=BS), :]
                        for part in range(natural.shape[0])
                    ],
                    axis=1,
                )
            )
    mixed = jnp.concatenate(order, axis=0)
    border[...] = mm3(split(dense_ref[...]), split(mixed), TN)
    per = outs[0].shape[0]
    for s in range(members):
        outs[s][...] = border[rows_at(lax.bitwise_xor(me, s), per), :]


def collect(members, list_ref, weight_ref, *refs):
    pieces, out_ref, border = refs[:members], refs[members], refs[members + 1]
    me = lax.axis_index("row")
    per = pieces[0].shape[0]
    for s in range(members):
        border[rows_at(lax.bitwise_xor(me, s), per), :] = pieces[s][...]
    pick = one_hot(list_ref, me, border.shape[0], out_ref.shape[0])
    high, low = split(border[...])
    proj = mm(pick, high, NN) + mm(pick, low, NN)
    out_ref[...] = mm3(split(proj), split(weight_ref[...]), NT)


def finish(members, *refs):
    pieces, weight_ref, bias_ref = refs[:members], refs[members], refs[members + 1]
    me = lax.axis_index("row")
    chunk = pieces[0].shape[0] - PAD
    total = pieces[0][chunk : chunk + 1, :]
    for s in range(members):
        weight_ref[rows_at(lax.bitwise_xor(me, s), chunk), :] = pieces[s][0:chunk, :]
        if s:
            total = total + pieces[s][chunk : chunk + 1, :]
    bias_ref[...] = total


def exchange(value, axis, shift):
    size = lax.axis_size(axis)
    return lax.ppermute(value, axis, [(i, i ^ shift) for i in range(size)])


def per_device(
    node_feat, weight, bias, cotangent, blocks, row_block, col_block, live_blocks, send_list
):
    nodes, width = node_feat.shape
    groups, members = lax.axis_size("rep"), lax.axis_size("row")
    capacity = blocks.shape[2]
    per = send_list.shape[-1] // (members * members)
    slots = members * per
    row_blocks = groups * nodes // BS
    col_blocks = slots // BS
    rows = row_blocks * BS
    shape = lambda n: jax.ShapeDtypeStruct((n, width), F32)
    vmem = lambda n: pltpu.VMEM((n, width), F32)
    tiles = pltpu.VMEM((width // LANES, rows, LANES), F32)

    sends = call(
        functools.partial(gather_rows, members),
        [shape(per)] * members,
        [send_list, node_feat],
        [vmem(slots)],
    )
    border = [sends[0]] + [exchange(sends[s], "row", s) for s in range(1, members)]
    dense = pl.pallas_call(
        functools.partial(build_one, row_blocks, col_blocks),
        out_shape=jax.ShapeDtypeStruct((rows, slots), F32),
        in_specs=[
            pl.BlockSpec(memory_space=pltpu.SMEM),
            pl.BlockSpec(memory_space=pltpu.VMEM),
            pl.BlockSpec(memory_space=pltpu.VMEM),
            pl.BlockSpec(memory_space=pltpu.VMEM),
        ],
        out_specs=pl.BlockSpec(memory_space=pltpu.VMEM),
        cost_estimate=pl.CostEstimate(
            flops=4 * row_blocks * col_blocks * capacity * BS * BS,
            transcendentals=0,
            bytes_accessed=8 * capacity * BS * BS,
        ),
        name="build",
    )(live_blocks, row_block[0], col_block[0], blocks[0, 0])
    partials = call(
        functools.partial(aggregate, members, groups, row_blocks),
        [shape(nodes)] * groups,
        [dense] + border,
        [vmem(slots), tiles],
        flops=6 * rows * slots * width,
    )
    parts = [partials[0]] + [exchange(partials[s], "rep", s) for s in range(1, groups)]
    activated, grad, keep, send, bias_part = call(
        functools.partial(activate, groups, members),
        [shape(nodes), shape(nodes), shape(width // 2), shape(width // 2), shape(PAD)],
        parts + [weight, bias[None, :], cotangent],
        [vmem(width)],
        flops=12 * nodes * width * width,
    )
    grads = [grad] + [exchange(grad, "rep", s) for s in range(1, groups)]
    backs = call(
        functools.partial(spread, groups, members, row_blocks),
        [shape(per)] * members,
        [dense] + grads,
        [tiles, vmem(slots)],
        flops=6 * rows * slots * width,
    )
    returned = [backs[0]] + [exchange(backs[s], "row", s) for s in range(1, members)]
    (feat_grad,) = call(
        functools.partial(collect, members),
        [shape(nodes)],
        [send_list, weight] + returned,
        [vmem(slots)],
        flops=6 * nodes * width * width,
    )
    shift = 1
    while shift < members:
        total = keep + exchange(send, "row", shift)
        shift *= 2
        if shift < members:
            half = total.shape[0] // 2
            keep, send = total[:half], total[half:]
    chunk = jnp.concatenate([total, bias_part], axis=0)
    summed = chunk
    for s in range(1, groups):
        summed = summed + exchange(chunk, "rep", s)
    chunks = [summed]
    for s in range(1, members):
        chunks.append(exchange(summed, "row", s) if s % 2 == 0 else None)
    for s in range(1, members, 2):
        chunks[s] = exchange(chunks[s - 1], "row", 1)
    weight_grad, bias_grad = call(
        functools.partial(finish, members), [shape(width), shape(1)], chunks
    )
    return (activated, feat_grad, weight_grad, bias_grad[0])


def build_one(row_blocks, col_blocks, live_ref, rows_ref, cols_ref, blocks_ref, out_ref):
    capacity = blocks_ref.shape[0]
    pairs = row_blocks * col_blocks
    steps = blocks_ref.shape[1] // LANES
    pair_of = cols_ref[...] * row_blocks + rows_ref[...]
    pair = lax.broadcasted_iota(jnp.int32, (pairs, capacity), 0)
    slot = lax.broadcasted_iota(jnp.int32, (pairs, capacity), 1)
    pick = ((pair == pair_of) & (slot < live_ref[0, 0])).astype(BF16)
    high, low = split(blocks_ref[...])
    dense = mm(pick, high, NN) + mm(pick, low, NN)
    left = lax.broadcasted_iota(jnp.int32, (row_blocks, LANES), 1) < BS
    for t in range(steps):
        lanes = slice(t * LANES, (t + 1) * LANES)
        for u in range(col_blocks // 2):
            first = dense[2 * u * row_blocks : (2 * u + 1) * row_blocks, lanes]
            second = dense[(2 * u + 1) * row_blocks : (2 * u + 2) * row_blocks, lanes]
            even = jnp.where(left, first, pltpu.roll(second, BS, 1))
            odd = jnp.where(left, pltpu.roll(first, BS, 1), second)
            for parity, value in ((0, even), (1, odd)):
                start = (parity * steps + t) * row_blocks
                out_ref[start : start + row_blocks, u * LANES : (u + 1) * LANES] = value


def solution(mesh):
    return jax.shard_map(
        per_device,
        mesh=mesh,
        in_specs=(
            P(("rep", "row"), None),
            P(),
            P(),
            P(("rep", "row"), None),
            P("rep", "row", None, None),
            P("rep", "row", None),
            P("rep", "row", None),
            P("rep", "row"),
            P("rep", None),
        ),
        out_specs=(P(("rep", "row"), None), P(("rep", "row"), None), P(), P()),
        check_vma=False,
    )
```

```python
import functools

import jax
import jax.numpy as jnp
from jax import lax
from jax.experimental import pallas as pl
from jax.experimental.pallas import tpu as pltpu
from jax.sharding import PartitionSpec as P

BS = 64
LANES = 128
PAD = 8
FLOOR = 16 * 2**20
F32 = jnp.float32
BF16 = jnp.bfloat16
NN = (((1,), (0,)), ((), ()))
TN = (((0,), (0,)), ((), ()))
NT = (((1,), (1,)), ((), ()))


def split(x):
    high = x.astype(BF16)
    return high, (x - high.astype(F32)).astype(BF16)


def mm(a, b, dims):
    return lax.dot_general(a, b, dims, preferred_element_type=F32)


def mm3(a, b, dims):
    return mm(a[0], b[0], dims) + (mm(a[0], b[1], dims) + mm(a[1], b[0], dims))


def call(kernel, outs, args, scratch=(), flops=0, smem=()):
    out_bytes = sum(int(o.size) * o.dtype.itemsize for o in outs)
    in_bytes = sum(int(a.size) * a.dtype.itemsize for a in args)
    limit = max(FLOOR, 6 * (in_bytes + out_bytes))
    return pl.pallas_call(
        kernel,
        out_shape=outs,
        in_specs=[
            pl.BlockSpec(memory_space=pltpu.SMEM if k in smem else pltpu.VMEM)
            for k in range(len(args))
        ],
        out_specs=[pl.BlockSpec(memory_space=pltpu.VMEM) for _ in outs],
        scratch_shapes=list(scratch),
        cost_estimate=pl.CostEstimate(
            flops=flops, transcendentals=0, bytes_accessed=in_bytes + out_bytes
        ),
        compiler_params=pltpu.CompilerParams(vmem_limit_bytes=limit),
        name=kernel.func.__name__ if hasattr(kernel, "func") else kernel.__name__,
    )(*args)


def rows_at(index, count):
    return pl.ds(pl.multiple_of(index * count, count), count)


def one_hot(list_ref, me, slots, nodes):
    wanted = list_ref[:, rows_at(me, slots)]
    node = lax.broadcasted_iota(jnp.int32, (nodes, slots), 0)
    return (node == wanted).astype(BF16)


def gather_rows(members, list_ref, feat_ref, *refs):
    outs, buffer = refs[:-1], refs[-1]
    me = lax.axis_index("row")
    nodes = feat_ref.shape[0]
    slots = buffer.shape[0]
    pick = one_hot(list_ref, me, slots, nodes)
    high, low = split(feat_ref[...])
    buffer[...] = mm(pick, high, TN) + mm(pick, low, TN)
    for s in range(members):
        outs[s][...] = buffer[rows_at(lax.bitwise_xor(me, s), slots // members), :]


def aggregate(me_count, groups, row_blocks, dense_ref, *refs):
    pieces, outs = refs[:me_count], refs[me_count : me_count + groups]
    border, natural = refs[me_count + groups :]
    me, group = lax.axis_index("row"), lax.axis_index("rep")
    per = pieces[0].shape[0]
    for s in range(me_count):
        border[rows_at(lax.bitwise_xor(me, s), per), :] = pieces[s][...]
    result = mm3(split(dense_ref[...]), split(border[...]), NN)
    unmix(result, natural, row_blocks)
    nodes = outs[0].shape[0]
    for s in range(groups):
        for part in range(natural.shape[0]):
            outs[s][:, part * LANES : (part + 1) * LANES] = natural[
                part, rows_at(lax.bitwise_xor(group, s), nodes), :
            ]


def unmix(result, natural, row_blocks):
    for m in range(BS):
        start = ((m % 2) * (BS // 2) + m // 2) * row_blocks
        for part in range(natural.shape[0]):
            natural[part, pl.ds(m, row_blocks, stride=BS), :] = result[
                start : start + row_blocks, part * LANES : (part + 1) * LANES
            ]


def activate(groups, members, *refs):
    pieces = refs[:groups]
    weight_ref, bias_ref, cot_ref, act_ref, grad_ref, keep_ref, send_ref, part_ref, buffer = refs[groups:]
    me = lax.axis_index("row")
    total = pieces[0][...]
    for s in range(1, groups):
        total = total + pieces[s][...]
    total_split = split(total)
    pre = mm3(total_split, split(weight_ref[...]), NN) + bias_ref[...]
    gate = jax.nn.sigmoid(pre)
    act_ref[...] = pre * gate
    grad = cot_ref[...] * (gate * (1.0 + pre * (1.0 - gate)))
    grad_ref[...] = grad
    buffer[...] = mm3(total_split, split(grad), TN)
    half = members // 2
    chunk = buffer.shape[0] // members
    bits = members.bit_length() - 1
    for k in range(members):
        s = int(format(k, f"0{bits}b")[::-1], 2)
        value = buffer[rows_at(lax.bitwise_xor(me, s), chunk), :]
        target = keep_ref if k < half else send_ref
        k = k % half
        target[k * chunk : (k + 1) * chunk, :] = value
    sums = jnp.sum(grad, axis=0, keepdims=True)
    part_ref[...] = jnp.broadcast_to(sums, part_ref.shape)


def spread(groups, members, row_blocks, dense_ref, *refs):
    pieces, outs = refs[:groups], refs[groups : groups + members]
    natural, border = refs[groups + members :]
    me, group = lax.axis_index("row"), lax.axis_index("rep")
    nodes = pieces[0].shape[0]
    for s in range(groups):
        for part in range(natural.shape[0]):
            natural[part, rows_at(lax.bitwise_xor(group, s), nodes), :] = pieces[s][
                :, part * LANES : (part + 1) * LANES
            ]
    order = []
    for parity in range(2):
        for t in range(BS // 2):
            order.append(
                jnp.concatenate(
                    [
                        natural[part, pl.ds(2 * t + parity, row_blocks, stride=BS), :]
                        for part in range(natural.shape[0])
                    ],
                    axis=1,
                )
            )
    mixed = jnp.concatenate(order, axis=0)
    border[...] = mm3(split(dense_ref[...]), split(mixed), TN)
    per = outs[0].shape[0]
    for s in range(members):
        outs[s][...] = border[rows_at(lax.bitwise_xor(me, s), per), :]


def collect(members, list_ref, weight_ref, *refs):
    pieces, out_ref, border = refs[:members], refs[members], refs[members + 1]
    me = lax.axis_index("row")
    per = pieces[0].shape[0]
    for s in range(members):
        border[rows_at(lax.bitwise_xor(me, s), per), :] = pieces[s][...]
    pick = one_hot(list_ref, me, border.shape[0], out_ref.shape[0])
    high, low = split(border[...])
    proj = mm(pick, high, NN) + mm(pick, low, NN)
    out_ref[...] = mm3(split(proj), split(weight_ref[...]), NT)


def finish(members, *refs):
    pieces, weight_ref, bias_ref = refs[:members], refs[members], refs[members + 1]
    me = lax.axis_index("row")
    chunk = pieces[0].shape[0] - PAD
    total = pieces[0][chunk : chunk + 1, :]
    for s in range(members):
        weight_ref[rows_at(lax.bitwise_xor(me, s), chunk), :] = pieces[s][0:chunk, :]
        if s:
            total = total + pieces[s][chunk : chunk + 1, :]
    bias_ref[...] = total


def exchange(value, axis, shift):
    size = lax.axis_size(axis)
    return lax.ppermute(value, axis, [(i, i ^ shift) for i in range(size)])


def per_device(
    node_feat, weight, bias, cotangent, blocks, row_block, col_block, live_blocks, send_list
):
    nodes, width = node_feat.shape
    groups, members = lax.axis_size("rep"), lax.axis_size("row")
    capacity = blocks.shape[2]
    per = send_list.shape[-1] // (members * members)
    slots = members * per
    row_blocks = groups * nodes // BS
    col_blocks = slots // BS
    rows = row_blocks * BS
    shape = lambda n: jax.ShapeDtypeStruct((n, width), F32)
    vmem = lambda n: pltpu.VMEM((n, width), F32)
    tiles = pltpu.VMEM((width // LANES, rows, LANES), F32)

    sends = call(
        functools.partial(gather_rows, members),
        [shape(per)] * members,
        [send_list, node_feat],
        [vmem(slots)],
    )
    border = [sends[0]] + [exchange(sends[s], "row", s) for s in range(1, members)]
    dense = pl.pallas_call(
        functools.partial(build_one, row_blocks, col_blocks),
        out_shape=jax.ShapeDtypeStruct((rows, slots), F32),
        in_specs=[
            pl.BlockSpec(memory_space=pltpu.SMEM),
            pl.BlockSpec(memory_space=pltpu.VMEM),
            pl.BlockSpec(memory_space=pltpu.VMEM),
            pl.BlockSpec(memory_space=pltpu.VMEM),
        ],
        out_specs=pl.BlockSpec(memory_space=pltpu.VMEM),
        cost_estimate=pl.CostEstimate(
            flops=4 * row_blocks * col_blocks * capacity * BS * BS,
            transcendentals=0,
            bytes_accessed=8 * capacity * BS * BS,
        ),
        compiler_params=pltpu.CompilerParams(
            vmem_limit_bytes=max(FLOOR, 8 * capacity * BS * BS * 4 + 12 * rows * slots)
        ),
        name="build",
    )(live_blocks, row_block[0], col_block[0], blocks[0, 0])
    partials = call(
        functools.partial(aggregate, members, groups, row_blocks),
        [shape(nodes)] * groups,
        [dense] + border,
        [vmem(slots), tiles],
        flops=6 * rows * slots * width,
    )
    parts = [partials[0]] + [exchange(partials[s], "rep", s) for s in range(1, groups)]
    activated, grad, keep, send, bias_part = call(
        functools.partial(activate, groups, members),
        [shape(nodes), shape(nodes), shape(width // 2), shape(width // 2), shape(PAD)],
        parts + [weight, bias[None, :], cotangent],
        [vmem(width)],
        flops=12 * nodes * width * width,
    )
    grads = [grad] + [exchange(grad, "rep", s) for s in range(1, groups)]
    backs = call(
        functools.partial(spread, groups, members, row_blocks),
        [shape(per)] * members,
        [dense] + grads,
        [tiles, vmem(slots)],
        flops=6 * rows * slots * width,
    )
    returned = [backs[0]] + [exchange(backs[s], "row", s) for s in range(1, members)]
    (feat_grad,) = call(
        functools.partial(collect, members),
        [shape(nodes)],
        [send_list, weight] + returned,
        [vmem(slots)],
        flops=6 * nodes * width * width,
    )
    shift = 1
    while shift < members:
        total = keep + exchange(send, "row", shift)
        shift *= 2
        if shift < members:
            half = total.shape[0] // 2
            keep, send = total[:half], total[half:]
    chunk = jnp.concatenate([total, bias_part], axis=0)
    summed = chunk
    for s in range(1, groups):
        summed = summed + exchange(chunk, "rep", s)
    chunks = [summed]
    for s in range(1, members):
        chunks.append(exchange(summed, "row", s) if s % 2 == 0 else None)
    for s in range(1, members, 2):
        chunks[s] = exchange(chunks[s - 1], "row", 1)
    weight_grad, bias_grad = call(
        functools.partial(finish, members), [shape(width), shape(1)], chunks
    )
    return (activated, feat_grad, weight_grad, bias_grad[0])


def build_one(row_blocks, col_blocks, live_ref, rows_ref, cols_ref, blocks_ref, out_ref):
    capacity = blocks_ref.shape[0]
    pairs = row_blocks * col_blocks
    steps = blocks_ref.shape[1] // LANES
    pair_of = cols_ref[...] * row_blocks + rows_ref[...]
    pair = lax.broadcasted_iota(jnp.int32, (pairs, capacity), 0)
    slot = lax.broadcasted_iota(jnp.int32, (pairs, capacity), 1)
    pick = ((pair == pair_of) & (slot < live_ref[0, 0])).astype(BF16)
    high, low = split(blocks_ref[...])
    dense = mm(pick, high, NN) + mm(pick, low, NN)
    left = lax.broadcasted_iota(jnp.int32, (row_blocks, LANES), 1) < BS
    for t in range(steps):
        lanes = slice(t * LANES, (t + 1) * LANES)
        for u in range(col_blocks // 2):
            first = dense[2 * u * row_blocks : (2 * u + 1) * row_blocks, lanes]
            second = dense[(2 * u + 1) * row_blocks : (2 * u + 2) * row_blocks, lanes]
            even = jnp.where(left, first, pltpu.roll(second, BS, 1))
            odd = jnp.where(left, pltpu.roll(first, BS, 1), second)
            for parity, value in ((0, even), (1, odd)):
                start = (parity * steps + t) * row_blocks
                out_ref[start : start + row_blocks, u * LANES : (u + 1) * LANES] = value


def solution(mesh):
    return jax.shard_map(
        per_device,
        mesh=mesh,
        in_specs=(
            P(("rep", "row"), None),
            P(),
            P(),
            P(("rep", "row"), None),
            P("rep", "row", None, None),
            P("rep", "row", None),
            P("rep", "row", None),
            P("rep", "row"),
            P("rep", None),
        ),
        out_specs=(P(("rep", "row"), None), P(("rep", "row"), None), P(), P()),
        check_vma=False,
    )
```

```python
import functools

import jax
import jax.numpy as jnp
from jax import lax
from jax.experimental import pallas as pl
from jax.experimental.pallas import tpu as pltpu
from jax.sharding import PartitionSpec as P


BS = 64
LANES = 128
PAD = 8
FLOOR = 16 * 2**20
F32 = jnp.float32
BF16 = jnp.bfloat16
NN = (((1,), (0,)), ((), ()))
TN = (((0,), (0,)), ((), ()))
NT = (((1,), (1,)), ((), ()))


def split(x):
    high = x.astype(BF16)
    return high, (x - high.astype(F32)).astype(BF16)


def mm(a, b, dims):
    return lax.dot_general(a, b, dims, preferred_element_type=F32)


def mm3(a, b, dims):
    return mm(a[0], b[0], dims) + (mm(a[0], b[1], dims) + mm(a[1], b[0], dims))


def call(kernel, outs, args, scratch=(), flops=0, smem=()):
    out_bytes = sum(int(o.size) * o.dtype.itemsize for o in outs)
    in_bytes = sum(int(a.size) * a.dtype.itemsize for a in args)
    limit = max(FLOOR, 6 * (in_bytes + out_bytes))
    return pl.pallas_call(
        kernel,
        out_shape=outs,
        in_specs=[
            pl.BlockSpec(memory_space=pltpu.SMEM if k in smem else pltpu.VMEM)
            for k in range(len(args))
        ],
        out_specs=[pl.BlockSpec(memory_space=pltpu.VMEM) for _ in outs],
        scratch_shapes=list(scratch),
        cost_estimate=pl.CostEstimate(
            flops=flops, transcendentals=0, bytes_accessed=in_bytes + out_bytes
        ),
        compiler_params=pltpu.CompilerParams(vmem_limit_bytes=limit),
    )(*args)


def rows_at(index, count):
    return pl.ds(pl.multiple_of(index * count, count), count)


def one_hot(list_ref, me, slots, nodes):
    wanted = list_ref[:, rows_at(me, slots)]
    node = lax.broadcasted_iota(jnp.int32, (nodes, slots), 0)
    return (node == wanted).astype(BF16)


def put_pairs(outs, buffer, me, per):
    for pair, out in enumerate(outs):
        for core in range(2):
            source = rows_at(lax.bitwise_xor(me, 2 * pair + core), per)
            out[core * per : (core + 1) * per, :] = buffer[source, :]


def take_pairs(own_ref, partner_ref, buffer, me, per):
    for pair in range(buffer.shape[0] // (2 * per)):
        rows = slice(pair * per, (pair + 1) * per)
        buffer[rows_at(lax.bitwise_xor(me, 2 * pair), per), :] = own_ref[rows, :]
        buffer[rows_at(lax.bitwise_xor(me, 2 * pair + 1), per), :] = partner_ref[rows, :]


def gather_rows(list_ref, feat_ref, *refs):
    outs, buffer = refs[:-1], refs[-1]
    me = lax.axis_index("row")
    nodes = feat_ref.shape[0]
    slots = buffer.shape[0]
    pick = one_hot(list_ref, me, slots, nodes)
    high, low = split(feat_ref[...])
    buffer[...] = mm(pick, high, TN) + mm(pick, low, TN)
    put_pairs(outs, buffer, me, outs[0].shape[0] // 2)


def aggregate(groups, row_blocks, per, dense_ref, own_ref, partner_ref, *refs):
    outs, border, natural = refs[:groups], refs[groups], refs[groups + 1]
    me, group = lax.axis_index("row"), lax.axis_index("rep")
    take_pairs(own_ref, partner_ref, border, me, per)
    result = mm3(split(dense_ref[...]), split(border[...]), NN)
    unmix(result, natural, row_blocks)
    nodes = outs[0].shape[0]
    for s in range(groups):
        for part in range(natural.shape[0]):
            outs[s][:, part * LANES : (part + 1) * LANES] = natural[
                part, rows_at(lax.bitwise_xor(group, s), nodes), :
            ]


def unmix(result, natural, row_blocks):
    for m in range(BS):
        start = ((m % 2) * (BS // 2) + m // 2) * row_blocks
        for part in range(natural.shape[0]):
            natural[part, pl.ds(m, row_blocks, stride=BS), :] = result[
                start : start + row_blocks, part * LANES : (part + 1) * LANES
            ]


def activate(groups, members, *refs):
    pieces = refs[:groups]
    weight_ref, bias_ref, cot_ref, act_ref, grad_ref, keep_ref, send_ref, part_ref, buffer = refs[groups:]
    me = lax.axis_index("row")
    total = pieces[0][...]
    for s in range(1, groups):
        total = total + pieces[s][...]
    total_split = split(total)
    pre = mm3(total_split, split(weight_ref[...]), NN) + bias_ref[...]
    gate = jax.nn.sigmoid(pre)
    act_ref[...] = pre * gate
    grad = cot_ref[...] * (gate * (1.0 + pre * (1.0 - gate)))
    grad_ref[...] = grad
    buffer[...] = mm3(total_split, split(grad), TN)
    half = members // 2
    chunk = buffer.shape[0] // members
    bits = members.bit_length() - 1
    for k in range(members):
        s = int(format(k, f"0{bits}b")[::-1], 2)
        value = buffer[rows_at(lax.bitwise_xor(me, s), chunk), :]
        target = keep_ref if k < half else send_ref
        k = k % half
        target[k * chunk : (k + 1) * chunk, :] = value
    sums = jnp.sum(grad, axis=0, keepdims=True)
    part_ref[...] = jnp.broadcast_to(sums, part_ref.shape)


def spread(groups, pairs, row_blocks, dense_ref, *refs):
    pieces, outs = refs[:groups], refs[groups : groups + pairs]
    natural, border = refs[groups + pairs :]
    me, group = lax.axis_index("row"), lax.axis_index("rep")
    nodes = pieces[0].shape[0]
    for s in range(groups):
        for part in range(natural.shape[0]):
            natural[part, rows_at(lax.bitwise_xor(group, s), nodes), :] = pieces[s][
                :, part * LANES : (part + 1) * LANES
            ]
    order = []
    for parity in range(2):
        for t in range(BS // 2):
            order.append(
                jnp.concatenate(
                    [
                        natural[part, pl.ds(2 * t + parity, row_blocks, stride=BS), :]
                        for part in range(natural.shape[0])
                    ],
                    axis=1,
                )
            )
    mixed = jnp.concatenate(order, axis=0)
    border[...] = mm3(split(dense_ref[...]), split(mixed), TN)
    put_pairs(outs, border, me, outs[0].shape[0] // 2)


def collect(per, list_ref, weight_ref, own_ref, partner_ref, out_ref, border):
    me = lax.axis_index("row")
    take_pairs(own_ref, partner_ref, border, me, per)
    pick = one_hot(list_ref, me, border.shape[0], out_ref.shape[0])
    high, low = split(border[...])
    proj = mm(pick, high, NN) + mm(pick, low, NN)
    out_ref[...] = mm3(split(proj), split(weight_ref[...]), NT)


def finish(members, own_ref, partner_ref, weight_ref, bias_ref):
    me = lax.axis_index("row")
    step = own_ref.shape[0] // (members // 2)
    chunk = step - PAD
    total = jnp.zeros_like(bias_ref)
    for s in range(members):
        piece = partner_ref if s % 2 else own_ref
        start = (s // 2) * step
        weight_ref[rows_at(lax.bitwise_xor(me, s), chunk), :] = piece[start : start + chunk, :]
        total = total + piece[start + chunk : start + chunk + 1, :]
    bias_ref[...] = total


def exchange(value, axis, shift):
    size = lax.axis_size(axis)
    return lax.ppermute(value, axis, [(i, i ^ shift) for i in range(size)])


def swap_rows(sends):
    pieces = [sends[0]]
    pieces += [exchange(sends[p], "row", 2 * p) for p in range(1, len(sends))]
    per = sends[0].shape[0] // 2
    own = jnp.concatenate([piece[:per] for piece in pieces], axis=0)
    partner = jnp.concatenate([piece[per:] for piece in pieces], axis=0)
    return [own, exchange(partner, "row", 1)]


def layer(
    node_feat, weight, bias, cotangent, blocks, row_block, col_block, live_blocks, send_list
):
    nodes, width = node_feat.shape
    groups, members = lax.axis_size("rep"), lax.axis_size("row")
    capacity = blocks.shape[2]
    per = send_list.shape[-1] // (members * members)
    slots = members * per
    row_blocks = groups * nodes // BS
    col_blocks = slots // BS
    rows = row_blocks * BS
    pairs = members // 2
    shape = lambda n: jax.ShapeDtypeStruct((n, width), F32)
    vmem = lambda n: pltpu.VMEM((n, width), F32)
    tiles = pltpu.VMEM((width // LANES, rows, LANES), F32)

    sends = call(
        gather_rows,
        [shape(2 * per)] * pairs,
        [send_list, node_feat],
        [vmem(slots)],
    )
    border = swap_rows(sends)
    dense = pl.pallas_call(
        functools.partial(build_one, row_blocks, col_blocks),
        out_shape=jax.ShapeDtypeStruct((rows, slots), F32),
        in_specs=[
            pl.BlockSpec(memory_space=pltpu.SMEM),
            pl.BlockSpec(memory_space=pltpu.VMEM),
            pl.BlockSpec(memory_space=pltpu.VMEM),
            pl.BlockSpec(memory_space=pltpu.VMEM),
        ],
        out_specs=pl.BlockSpec(memory_space=pltpu.VMEM),
        cost_estimate=pl.CostEstimate(
            flops=4 * row_blocks * col_blocks * capacity * BS * BS,
            transcendentals=0,
            bytes_accessed=8 * capacity * BS * BS,
        ),
        compiler_params=pltpu.CompilerParams(
            vmem_limit_bytes=max(FLOOR, 8 * capacity * BS * BS * 4 + 12 * rows * slots)
        ),
        name="build",
    )(live_blocks, row_block[0], col_block[0], blocks[0, 0])
    partials = call(
        functools.partial(aggregate, groups, row_blocks, per),
        [shape(nodes)] * groups,
        [dense] + border,
        [vmem(slots), tiles],
        flops=6 * rows * slots * width,
    )
    parts = [partials[0]] + [exchange(partials[s], "rep", s) for s in range(1, groups)]
    activated, grad, keep, send, bias_part = call(
        functools.partial(activate, groups, members),
        [shape(nodes), shape(nodes), shape(width // 2), shape(width // 2), shape(PAD)],
        parts + [weight, bias[None, :], cotangent],
        [vmem(width)],
        flops=12 * nodes * width * width,
    )
    grads = [grad] + [exchange(grad, "rep", s) for s in range(1, groups)]
    backs = call(
        functools.partial(spread, groups, pairs, row_blocks),
        [shape(2 * per)] * pairs,
        [dense] + grads,
        [tiles, vmem(slots)],
        flops=6 * rows * slots * width,
    )
    returned = swap_rows(backs)
    (feat_grad,) = call(
        functools.partial(collect, per),
        [shape(nodes)],
        [send_list, weight] + returned,
        [vmem(slots)],
        flops=6 * nodes * width * width,
    )
    step = 0
    while 2**step < members:
        total = keep + exchange(send, "row", 2**step)
        step += 1
        if 2**step < members:
            half = total.shape[0] // 2
            keep, send = total[:half], total[half:]
    chunk = jnp.concatenate([total, bias_part], axis=0)
    summed = chunk
    for s in range(1, groups):
        summed = summed + exchange(chunk, "rep", s)
    chunks = [summed]
    chunks += [exchange(summed, "row", 2 * p) for p in range(1, pairs)]
    own = jnp.concatenate(chunks, axis=0)
    partner = exchange(own, "row", 1)
    weight_grad, bias_grad = call(
        functools.partial(finish, members), [shape(width), shape(1)], [own, partner]
    )
    return (activated, feat_grad, weight_grad, bias_grad[0])


def build_one(row_blocks, col_blocks, live_ref, rows_ref, cols_ref, blocks_ref, out_ref):
    capacity = blocks_ref.shape[0]
    pairs = row_blocks * col_blocks
    steps = blocks_ref.shape[1] // LANES
    pair_of = cols_ref[...] * row_blocks + rows_ref[...]
    pair = lax.broadcasted_iota(jnp.int32, (pairs, capacity), 0)
    slot = lax.broadcasted_iota(jnp.int32, (pairs, capacity), 1)
    pick = ((pair == pair_of) & (slot < live_ref[0, 0])).astype(BF16)
    high, low = split(blocks_ref[...])
    dense = mm(pick, high, NN) + mm(pick, low, NN)
    left = lax.broadcasted_iota(jnp.int32, (row_blocks, LANES), 1) < BS
    for t in range(steps):
        lanes = slice(t * LANES, (t + 1) * LANES)
        for u in range(col_blocks // 2):
            first = dense[2 * u * row_blocks : (2 * u + 1) * row_blocks, lanes]
            second = dense[(2 * u + 1) * row_blocks : (2 * u + 2) * row_blocks, lanes]
            even = jnp.where(left, first, pltpu.roll(second, BS, 1))
            odd = jnp.where(left, pltpu.roll(first, BS, 1), second)
            for parity, value in ((0, even), (1, odd)):
                start = (parity * steps + t) * row_blocks
                out_ref[start : start + row_blocks, u * LANES : (u + 1) * LANES] = value


def solution(mesh):
    return sharded(mesh)


def sharded(mesh):
    return jax.shard_map(
        layer,
        mesh=mesh,
        in_specs=(
            P(("rep", "row"), None),
            P(),
            P(),
            P(("rep", "row"), None),
            P("rep", "row", None, None),
            P("rep", "row", None),
            P("rep", "row", None),
            P("rep", "row"),
            P("rep", None),
        ),
        out_specs=(P(("rep", "row"), None), P(("rep", "row"), None), P(), P()),
        check_vma=False,
    )
```

```python
import functools

import jax
import jax.numpy as jnp
from jax import lax
from jax.experimental import pallas as pl
from jax.experimental.pallas import tpu as pltpu
from jax.sharding import PartitionSpec as P


BS = 64
LANES = 128
PAD = 8
FLOOR = 16 * 2**20
F32 = jnp.float32
BF16 = jnp.bfloat16
NN = (((1,), (0,)), ((), ()))
TN = (((0,), (0,)), ((), ()))
NT = (((1,), (1,)), ((), ()))


def split(x):
    high = x.astype(BF16)
    return high, (x - high.astype(F32)).astype(BF16)


def mm(a, b, dims):
    return lax.dot_general(a, b, dims, preferred_element_type=F32)


def mm3(a, b, dims):
    return mm(a[0], b[0], dims) + (mm(a[0], b[1], dims) + mm(a[1], b[0], dims))


def call(kernel, outs, args, scratch=(), flops=0, smem=(), hbm=()):
    out_bytes = sum(int(o.size) * o.dtype.itemsize for o in outs)
    in_bytes = sum(int(a.size) * a.dtype.itemsize for a in args)
    limit = max(FLOOR, 4 * (in_bytes + out_bytes))
    return pl.pallas_call(
        kernel,
        out_shape=outs,
        in_specs=[
            pl.BlockSpec(
                memory_space=pltpu.SMEM if k in smem else pltpu.HBM if k in hbm else pltpu.VMEM
            )
            for k in range(len(args))
        ],
        out_specs=[pl.BlockSpec(memory_space=pltpu.VMEM) for _ in outs],
        scratch_shapes=list(scratch),
        cost_estimate=pl.CostEstimate(
            flops=flops, transcendentals=0, bytes_accessed=in_bytes + out_bytes
        ),
        compiler_params=pltpu.CompilerParams(vmem_limit_bytes=limit),
    )(*args)


def rows_at(index, count):
    return pl.ds(pl.multiple_of(index * count, count), count)


def one_hot(wanted, nodes):
    node = lax.broadcasted_iota(jnp.int32, (nodes, wanted.shape[1]), 0)
    return (node == wanted).astype(BF16)


def tree_sum(terms):
    terms = list(terms)
    while len(terms) > 1:
        terms = [terms[k] + terms[k + 1] for k in range(0, len(terms), 2)]
    return terms[0]


def put_pairs(outs, buffer, me, per):
    for pair, out in enumerate(outs):
        for core in range(2):
            source = rows_at(lax.bitwise_xor(me, 2 * pair + core), per)
            out[core * per : (core + 1) * per, :] = buffer[source, :]


def take_pairs(own_ref, partner_ref, buffer, me, per):
    for pair in range(buffer.shape[0] // (2 * per)):
        rows = slice(pair * per, (pair + 1) * per)
        buffer[rows_at(lax.bitwise_xor(me, 2 * pair), per), :] = own_ref[rows, :]
        buffer[rows_at(lax.bitwise_xor(me, 2 * pair + 1), per), :] = partner_ref[rows, :]


def gather_rows(list_hbm, feat_hbm, *refs):
    outs, wanted_ref, feat_ref, buffer, sems = refs[:-4], refs[-4], refs[-3], refs[-2], refs[-1]
    me = lax.axis_index("row")
    slots = buffer.shape[0]
    copies = [
        pltpu.make_async_copy(feat_hbm, feat_ref, sems.at[0]),
        pltpu.make_async_copy(list_hbm.at[:, rows_at(me, slots)], wanted_ref, sems.at[1]),
    ]
    for copy in copies:
        copy.start()
    for copy in copies:
        copy.wait()
    pick = one_hot(wanted_ref[...], feat_ref.shape[0])
    high, low = split(feat_ref[...])
    buffer[...] = mm(pick, high, TN) + mm(pick, low, TN)
    put_pairs(outs, buffer, me, outs[0].shape[0] // 2)


def aggregate(groups, row_blocks, per, high_ref, low_ref, own_ref, partner_ref, *refs):
    outs, border, natural = refs[:groups], refs[groups], refs[groups + 1]
    me, group = lax.axis_index("row"), lax.axis_index("rep")
    take_pairs(own_ref, partner_ref, border, me, per)
    result = mm3((high_ref[...], low_ref[...]), split(border[...]), NN)
    unmix(result, natural, row_blocks)
    nodes = outs[0].shape[0]
    for s in range(groups):
        for part in range(natural.shape[0]):
            outs[s][:, part * LANES : (part + 1) * LANES] = natural[
                part, rows_at(lax.bitwise_xor(group, s), nodes), :
            ]


def unmix(result, natural, row_blocks):
    for m in range(BS):
        start = ((m % 2) * (BS // 2) + m // 2) * row_blocks
        for part in range(natural.shape[0]):
            natural[part, pl.ds(m, row_blocks, stride=BS), :] = result[
                start : start + row_blocks, part * LANES : (part + 1) * LANES
            ]


def activate(groups, members, *refs):
    pieces = refs[:groups]
    weight_ref, bias_ref, cot_ref, act_ref, grad_ref, keep_ref, send_ref, part_ref, buffer = refs[groups:]
    me = lax.axis_index("row")
    total = tree_sum([piece[...] for piece in pieces])
    total_split = split(total)
    pre = mm3(total_split, split(weight_ref[...]), NN) + bias_ref[...]
    gate = jax.nn.sigmoid(pre)
    act_ref[...] = pre * gate
    grad = cot_ref[...] * (gate * (1.0 + pre * (1.0 - gate)))
    grad_ref[...] = grad
    buffer[...] = mm3(total_split, split(grad), TN)
    chunk = buffer.shape[0] // members
    for s in range(members):
        target = send_ref if s % 2 else keep_ref
        start = (s // 2) * chunk
        target[start : start + chunk, :] = buffer[rows_at(lax.bitwise_xor(me, s), chunk), :]
    sums = jnp.sum(grad, axis=0, keepdims=True)
    part_ref[...] = jnp.broadcast_to(sums, part_ref.shape)


def spread(groups, pairs, row_blocks, high_ref, low_ref, *refs):
    pieces, outs = refs[:groups], refs[groups : groups + pairs]
    natural, border = refs[groups + pairs :]
    me, group = lax.axis_index("row"), lax.axis_index("rep")
    nodes = pieces[0].shape[0]
    for s in range(groups):
        for part in range(natural.shape[0]):
            natural[part, rows_at(lax.bitwise_xor(group, s), nodes), :] = pieces[s][
                :, part * LANES : (part + 1) * LANES
            ]
    order = []
    for parity in range(2):
        for t in range(BS // 2):
            order.append(
                jnp.concatenate(
                    [
                        natural[part, pl.ds(2 * t + parity, row_blocks, stride=BS), :]
                        for part in range(natural.shape[0])
                    ],
                    axis=1,
                )
            )
    mixed = jnp.concatenate(order, axis=0)
    border[...] = mm3((high_ref[...], low_ref[...]), split(mixed), NN)
    put_pairs(outs, border, me, outs[0].shape[0] // 2)


def collect(per, wanted_ref, weight_ref, own_ref, partner_ref, out_ref, border):
    me = lax.axis_index("row")
    take_pairs(own_ref, partner_ref, border, me, per)
    pick = one_hot(wanted_ref[...], out_ref.shape[0])
    high, low = split(border[...])
    proj = mm(pick, high, NN) + mm(pick, low, NN)
    out_ref[...] = mm3(split(proj), split(weight_ref[...]), NT)


def finish(members, own_ref, partner_ref, weight_ref, bias_ref):
    me = lax.axis_index("row")
    step = own_ref.shape[0] // (members // 2)
    chunk = step - PAD
    terms = []
    for s in range(members):
        piece = partner_ref if s % 2 else own_ref
        start = (s // 2) * step
        weight_ref[rows_at(lax.bitwise_xor(me, s), chunk), :] = piece[start : start + chunk, :]
        terms.append(piece[start + chunk : start + chunk + 1, :])
    bias_ref[...] = tree_sum(terms)


def exchange(value, axis, shift):
    size = lax.axis_size(axis)
    return lax.ppermute(value, axis, [(i, i ^ shift) for i in range(size)])


def swap_rows(sends):
    pieces = [sends[0]]
    pieces += [exchange(sends[p], "row", 2 * p) for p in range(1, len(sends))]
    per = sends[0].shape[0] // 2
    own = jnp.concatenate([piece[:per] for piece in pieces], axis=0)
    partner = jnp.concatenate([piece[per:] for piece in pieces], axis=0)
    return [own, exchange(partner, "row", 1)]


def layer(
    node_feat, weight, bias, cotangent, blocks, row_block, col_block, live_blocks, send_list
):
    nodes, width = node_feat.shape
    groups, members = lax.axis_size("rep"), lax.axis_size("row")
    capacity = blocks.shape[2]
    per = send_list.shape[-1] // (members * members)
    slots = members * per
    row_blocks = groups * nodes // BS
    col_blocks = slots // BS
    rows = row_blocks * BS
    pairs = members // 2
    shape = lambda n: jax.ShapeDtypeStruct((n, width), F32)
    vmem = lambda n: pltpu.VMEM((n, width), F32)
    tiles = pltpu.VMEM((width // LANES, rows, LANES), F32)

    *sends, wanted = call(
        gather_rows,
        [shape(2 * per)] * pairs + [jax.ShapeDtypeStruct((1, slots), jnp.int32)],
        [pltpu.with_memory_space_constraint(x, pltpu.HBM) for x in (send_list, node_feat)],
        [vmem(nodes), vmem(slots), pltpu.SemaphoreType.DMA((2,))],
        hbm=(0, 1),
    )
    border = swap_rows(sends)
    wide = jax.ShapeDtypeStruct((rows, slots), BF16)
    tall = jax.ShapeDtypeStruct((slots, rows), BF16)
    bias_row = jax.ShapeDtypeStruct((1, width), F32)
    *dense, bias_here = call(
        functools.partial(build, row_blocks, col_blocks),
        [wide, wide, tall, tall, bias_row],
        [live_blocks, row_block[0], col_block[0], blocks[0, 0], bias[None, :]],
        [pltpu.VMEM((rows, slots), F32)],
        flops=4 * row_blocks * col_blocks * capacity * BS * BS,
        smem=(0,),
    )
    partials = call(
        functools.partial(aggregate, groups, row_blocks, per),
        [shape(nodes)] * groups,
        dense[:2] + border,
        [vmem(slots), tiles],
        flops=6 * rows * slots * width,
    )
    parts = [partials[0]] + [exchange(partials[s], "rep", s) for s in range(1, groups)]
    activated, grad, keep, send, bias_part = call(
        functools.partial(activate, groups, members),
        [shape(nodes), shape(nodes), shape(width // 2), shape(width // 2), shape(PAD)],
        parts + [weight, bias_here, cotangent],
        [vmem(width)],
        flops=12 * nodes * width * width,
    )
    grads = [grad] + [exchange(grad, "rep", s) for s in range(1, groups)]
    backs = call(
        functools.partial(spread, groups, pairs, row_blocks),
        [shape(2 * per)] * pairs,
        dense[2:] + grads,
        [tiles, vmem(slots)],
        flops=6 * rows * slots * width,
    )
    returned = swap_rows(backs)
    (feat_grad,) = call(
        functools.partial(collect, per),
        [shape(nodes)],
        [wanted, weight] + returned,
        [vmem(slots)],
        flops=6 * nodes * width * width,
    )
    total = keep + exchange(send, "row", 1)
    size = width // members
    owned = [total[p * size : (p + 1) * size] for p in range(pairs)]
    owned[1:] = [exchange(owned[p], "row", 2 * p) for p in range(1, pairs)]
    chunk = jnp.concatenate([tree_sum(owned), bias_part], axis=0)
    summed = tree_sum([chunk] + [exchange(chunk, "rep", s) for s in range(1, groups)])
    chunks = [summed]
    chunks += [exchange(summed, "row", 2 * p) for p in range(1, pairs)]
    own = jnp.concatenate(chunks, axis=0)
    partner = exchange(own, "row", 1)
    weight_grad, bias_grad = call(
        functools.partial(finish, members), [shape(width), shape(1)], [own, partner]
    )
    return (activated, feat_grad, weight_grad, bias_grad[0])


def build(row_blocks, col_blocks, live_ref, rows_ref, cols_ref, blocks_ref, bias_ref, *refs):
    high_ref, low_ref, high_t_ref, low_t_ref, bias_out, out_ref = refs
    bias_out[...] = bias_ref[...]
    capacity = blocks_ref.shape[0]
    pairs = row_blocks * col_blocks
    steps = blocks_ref.shape[1] // LANES
    pair_of = cols_ref[...] * row_blocks + rows_ref[...]
    pair = lax.broadcasted_iota(jnp.int32, (pairs, capacity), 0)
    slot = lax.broadcasted_iota(jnp.int32, (pairs, capacity), 1)
    pick = ((pair == pair_of) & (slot < live_ref[0, 0])).astype(BF16)
    high, low = split(blocks_ref[...])
    dense = mm(pick, high, NN) + mm(pick, low, NN)
    left = lax.broadcasted_iota(jnp.int32, (row_blocks, LANES), 1) < BS
    for t in range(steps):
        lanes = slice(t * LANES, (t + 1) * LANES)
        for u in range(col_blocks // 2):
            first = dense[2 * u * row_blocks : (2 * u + 1) * row_blocks, lanes]
            second = dense[(2 * u + 1) * row_blocks : (2 * u + 2) * row_blocks, lanes]
            even = jnp.where(left, first, pltpu.roll(second, BS, 1))
            odd = jnp.where(left, pltpu.roll(first, BS, 1), second)
            for parity, value in ((0, even), (1, odd)):
                start = (parity * steps + t) * row_blocks
                out_ref[start : start + row_blocks, u * LANES : (u + 1) * LANES] = value
    full = out_ref[...]
    high_ref[...], low_ref[...] = split(full)
    high_t_ref[...], low_t_ref[...] = split(full.T)


def solution(mesh):
    return sharded(mesh)


def sharded(mesh):
    return jax.shard_map(
        layer,
        mesh=mesh,
        in_specs=(
            P(("rep", "row"), None),
            P(),
            P(),
            P(("rep", "row"), None),
            P("rep", "row", None, None),
            P("rep", "row", None),
            P("rep", "row", None),
            P("rep", "row"),
            P("rep", None),
        ),
        out_specs=(P(("rep", "row"), None), P(("rep", "row"), None), P(), P()),
        check_vma=False,
    )
```

```python
import functools

import jax
import jax.numpy as jnp
from jax import lax
from jax.experimental import pallas as pl
from jax.experimental.pallas import tpu as pltpu
from jax.sharding import PartitionSpec as P


BS = 64
LANES = 128
PAD = 8
FLOOR = 16 * 2**20
F32 = jnp.float32
BF16 = jnp.bfloat16
NN = (((1,), (0,)), ((), ()))
TN = (((0,), (0,)), ((), ()))
NT = (((1,), (1,)), ((), ()))


def halvings(count):
    return [2**k for k in range(count.bit_length() - 1)]


def flipped(index, count):
    return sum(count // (2 * k) for k in halvings(count) if index & k)


def split(x):
    high = x.astype(BF16)
    return high, (x - high.astype(F32)).astype(BF16)


def mm(a, b, dims):
    return lax.dot_general(a, b, dims, preferred_element_type=F32)


def mm3(a, b, dims):
    return mm(a[0], b[0], dims) + (mm(a[0], b[1], dims) + mm(a[1], b[0], dims))


def call(kernel, outs, args, scratch=(), flops=0, smem=(), hbm=()):
    out_bytes = sum(int(o.size) * o.dtype.itemsize for o in outs)
    in_bytes = sum(int(a.size) * a.dtype.itemsize for a in args)
    limit = max(FLOOR, 4 * (in_bytes + out_bytes))
    return pl.pallas_call(
        kernel,
        out_shape=outs,
        in_specs=[
            pl.BlockSpec(
                memory_space=pltpu.SMEM if k in smem else pltpu.HBM if k in hbm else pltpu.VMEM
            )
            for k in range(len(args))
        ],
        out_specs=[pl.BlockSpec(memory_space=pltpu.VMEM) for _ in outs],
        scratch_shapes=list(scratch),
        cost_estimate=pl.CostEstimate(
            flops=flops, transcendentals=0, bytes_accessed=in_bytes + out_bytes
        ),
        compiler_params=pltpu.CompilerParams(vmem_limit_bytes=limit),
    )(*args)


def rows_at(index, count):
    return pl.ds(pl.multiple_of(index * count, count), count)


def one_hot(wanted, nodes):
    node = lax.broadcasted_iota(jnp.int32, (nodes, wanted.shape[1]), 0)
    return (node == wanted).astype(BF16)


def tree_sum(terms):
    terms = list(terms)
    while len(terms) > 1:
        terms = [terms[k] + terms[k + 1] for k in range(0, len(terms), 2)]
    return terms[0]


def put_pairs(outs, buffer, me, per):
    for pair, out in enumerate(outs):
        for core in range(2):
            source = rows_at(lax.bitwise_xor(me, 2 * pair + core), per)
            out[core * per : (core + 1) * per, :] = buffer[source, :]


def take_pairs(own_ref, partner_ref, buffer, me, per):
    for pair in range(buffer.shape[0] // (2 * per)):
        rows = slice(pair * per, (pair + 1) * per)
        buffer[rows_at(lax.bitwise_xor(me, 2 * pair), per), :] = own_ref[rows, :]
        buffer[rows_at(lax.bitwise_xor(me, 2 * pair + 1), per), :] = partner_ref[rows, :]


def gather_rows(list_hbm, feat_hbm, *refs):
    outs, wanted_ref, feat_ref, buffer, sems = refs[:-4], refs[-4], refs[-3], refs[-2], refs[-1]
    me = lax.axis_index("row")
    slots = buffer.shape[0]
    copies = [
        pltpu.make_async_copy(feat_hbm, feat_ref, sems.at[0]),
        pltpu.make_async_copy(list_hbm.at[:, rows_at(me, slots)], wanted_ref, sems.at[1]),
    ]
    for copy in copies:
        copy.start()
    for copy in copies:
        copy.wait()
    pick = one_hot(wanted_ref[...], feat_ref.shape[0])
    high, low = split(feat_ref[...])
    buffer[...] = mm(pick, high, TN) + mm(pick, low, TN)
    put_pairs(outs, buffer, me, outs[0].shape[0] // 2)


def aggregate(groups, row_blocks, per, high_ref, low_ref, own_ref, partner_ref, *refs):
    outs, border, natural = refs[:groups], refs[groups], refs[groups + 1]
    me, group = lax.axis_index("row"), lax.axis_index("rep")
    take_pairs(own_ref, partner_ref, border, me, per)
    result = mm3((high_ref[...], low_ref[...]), split(border[...]), NN)
    unmix(result, natural, row_blocks)
    nodes = outs[0].shape[0]
    for s in range(groups):
        for part in range(natural.shape[0]):
            outs[s][:, part * LANES : (part + 1) * LANES] = natural[
                part, rows_at(lax.bitwise_xor(group, s), nodes), :
            ]


def unmix(result, natural, row_blocks):
    for m in range(BS):
        start = ((m % 2) * (BS // 2) + m // 2) * row_blocks
        for part in range(natural.shape[0]):
            natural[part, pl.ds(m, row_blocks, stride=BS), :] = result[
                start : start + row_blocks, part * LANES : (part + 1) * LANES
            ]


def activate(groups, members, *refs):
    pieces = refs[:groups]
    weight_ref, bias_ref, cot_ref, act_ref, grad_ref, keep_ref, send_ref, part_ref, buffer = refs[groups:]
    me = lax.axis_index("row")
    total = tree_sum([piece[...] for piece in pieces])
    total_split = split(total)
    pre = mm3(total_split, split(weight_ref[...]), NN) + bias_ref[...]
    gate = jax.nn.sigmoid(pre)
    act_ref[...] = pre * gate
    grad = cot_ref[...] * (gate * (1.0 + pre * (1.0 - gate)))
    grad_ref[...] = grad
    buffer[...] = mm3(total_split, split(grad), TN)
    chunk = buffer.shape[0] // members
    for s in range(members):
        target = send_ref if s % 2 else keep_ref
        start = flipped(s // 2, members // 2) * chunk
        target[start : start + chunk, :] = buffer[rows_at(lax.bitwise_xor(me, s), chunk), :]
    sums = jnp.sum(grad, axis=0, keepdims=True)
    part_ref[...] = jnp.broadcast_to(sums, part_ref.shape)


def spread(groups, pairs, row_blocks, high_ref, low_ref, *refs):
    pieces, outs = refs[:groups], refs[groups : groups + pairs]
    natural, border = refs[groups + pairs :]
    me, group = lax.axis_index("row"), lax.axis_index("rep")
    nodes = pieces[0].shape[0]
    for s in range(groups):
        for part in range(natural.shape[0]):
            natural[part, rows_at(lax.bitwise_xor(group, s), nodes), :] = pieces[s][
                :, part * LANES : (part + 1) * LANES
            ]
    order = []
    for parity in range(2):
        for t in range(BS // 2):
            order.append(
                jnp.concatenate(
                    [
                        natural[part, pl.ds(2 * t + parity, row_blocks, stride=BS), :]
                        for part in range(natural.shape[0])
                    ],
                    axis=1,
                )
            )
    mixed = jnp.concatenate(order, axis=0)
    border[...] = mm3((high_ref[...], low_ref[...]), split(mixed), NN)
    put_pairs(outs, border, me, outs[0].shape[0] // 2)


def collect(per, wanted_ref, weight_ref, own_ref, partner_ref, out_ref, border):
    me = lax.axis_index("row")
    take_pairs(own_ref, partner_ref, border, me, per)
    pick = one_hot(wanted_ref[...], out_ref.shape[0])
    high, low = split(border[...])
    proj = mm(pick, high, NN) + mm(pick, low, NN)
    out_ref[...] = mm3(split(proj), split(weight_ref[...]), NT)


def finish(members, own_ref, partner_ref, weight_ref, bias_ref):
    me = lax.axis_index("row")
    step = own_ref.shape[0] // (members // 2)
    chunk = step - PAD
    terms = []
    for s in range(members):
        piece = partner_ref if s % 2 else own_ref
        start = flipped(s // 2, members // 2) * step
        weight_ref[rows_at(lax.bitwise_xor(me, s), chunk), :] = piece[start : start + chunk, :]
        terms.append(piece[start + chunk : start + chunk + 1, :])
    bias_ref[...] = tree_sum(terms)


def exchange(value, axis, shift):
    size = lax.axis_size(axis)
    return lax.ppermute(value, axis, [(i, i ^ shift) for i in range(size)])


def swap_rows(sends):
    pieces = [sends[0]]
    pieces += [exchange(sends[p], "row", 2 * p) for p in range(1, len(sends))]
    per = sends[0].shape[0] // 2
    own = jnp.concatenate([piece[:per] for piece in pieces], axis=0)
    partner = jnp.concatenate([piece[per:] for piece in pieces], axis=0)
    return [own, exchange(partner, "row", 1)]


def layer(
    node_feat, weight, bias, cotangent, blocks, row_block, col_block, live_blocks, send_list
):
    nodes, width = node_feat.shape
    groups, members = lax.axis_size("rep"), lax.axis_size("row")
    capacity = blocks.shape[2]
    per = send_list.shape[-1] // (members * members)
    slots = members * per
    row_blocks = groups * nodes // BS
    col_blocks = slots // BS
    rows = row_blocks * BS
    pairs = members // 2
    shape = lambda n: jax.ShapeDtypeStruct((n, width), F32)
    vmem = lambda n: pltpu.VMEM((n, width), F32)
    tiles = pltpu.VMEM((width // LANES, rows, LANES), F32)

    *sends, wanted = call(
        gather_rows,
        [shape(2 * per)] * pairs + [jax.ShapeDtypeStruct((1, slots), jnp.int32)],
        [pltpu.with_memory_space_constraint(x, pltpu.HBM) for x in (send_list, node_feat)],
        [vmem(nodes), vmem(slots), pltpu.SemaphoreType.DMA((2,))],
        hbm=(0, 1),
    )
    border = swap_rows(sends)
    wide = jax.ShapeDtypeStruct((rows, slots), BF16)
    tall = jax.ShapeDtypeStruct((slots, rows), BF16)
    bias_row = jax.ShapeDtypeStruct((1, width), F32)
    *dense, bias_here = call(
        functools.partial(build, row_blocks, col_blocks),
        [wide, wide, tall, tall, bias_row],
        [live_blocks, row_block[0], col_block[0], blocks[0, 0], bias[None, :]],
        [pltpu.VMEM((rows, slots), F32)],
        flops=4 * row_blocks * col_blocks * capacity * BS * BS,
        smem=(0,),
    )
    partials = call(
        functools.partial(aggregate, groups, row_blocks, per),
        [shape(nodes)] * groups,
        dense[:2] + border,
        [vmem(slots), tiles],
        flops=6 * rows * slots * width,
    )
    parts = [partials[0]] + [exchange(partials[s], "rep", s) for s in range(1, groups)]
    activated, grad, keep, send, bias_part = call(
        functools.partial(activate, groups, members),
        [shape(nodes), shape(nodes), shape(width // 2), shape(width // 2), shape(PAD)],
        parts + [weight, bias_here, cotangent],
        [vmem(width)],
        flops=12 * nodes * width * width,
    )
    grads = [grad] + [exchange(grad, "rep", s) for s in range(1, groups)]
    backs = call(
        functools.partial(spread, groups, pairs, row_blocks),
        [shape(2 * per)] * pairs,
        dense[2:] + grads,
        [tiles, vmem(slots)],
        flops=6 * rows * slots * width,
    )
    returned = swap_rows(backs)
    (feat_grad,) = call(
        functools.partial(collect, per),
        [shape(nodes)],
        [wanted, weight] + returned,
        [vmem(slots)],
        flops=6 * nodes * width * width,
    )
    total = keep + exchange(send, "row", 1)
    for step in halvings(pairs):
        half = total.shape[0] // 2
        total = total[:half] + exchange(total[half:], "row", 2 * step)
    total = jnp.concatenate([total, bias_part], axis=0)
    for step in halvings(groups):
        total = total + exchange(total, "rep", step)
    for step in reversed(halvings(pairs)):
        other = exchange(total, "row", 2 * step)
        total = jnp.concatenate([total, other], axis=0)
    partner = exchange(total, "row", 1)
    weight_grad, bias_grad = call(
        functools.partial(finish, members), [shape(width), shape(1)], [total, partner]
    )
    return (activated, feat_grad, weight_grad, bias_grad[0])


def build(row_blocks, col_blocks, live_ref, rows_ref, cols_ref, blocks_ref, bias_ref, *refs):
    high_ref, low_ref, high_t_ref, low_t_ref, bias_out, out_ref = refs
    bias_out[...] = bias_ref[...]
    capacity = blocks_ref.shape[0]
    pairs = row_blocks * col_blocks
    steps = blocks_ref.shape[1] // LANES
    pair_of = cols_ref[...] * row_blocks + rows_ref[...]
    pair = lax.broadcasted_iota(jnp.int32, (pairs, capacity), 0)
    slot = lax.broadcasted_iota(jnp.int32, (pairs, capacity), 1)
    pick = ((pair == pair_of) & (slot < live_ref[0, 0])).astype(BF16)
    high, low = split(blocks_ref[...])
    dense = mm(pick, high, NN) + mm(pick, low, NN)
    left = lax.broadcasted_iota(jnp.int32, (row_blocks, LANES), 1) < BS
    for t in range(steps):
        lanes = slice(t * LANES, (t + 1) * LANES)
        for u in range(col_blocks // 2):
            first = dense[2 * u * row_blocks : (2 * u + 1) * row_blocks, lanes]
            second = dense[(2 * u + 1) * row_blocks : (2 * u + 2) * row_blocks, lanes]
            even = jnp.where(left, first, pltpu.roll(second, BS, 1))
            odd = jnp.where(left, pltpu.roll(first, BS, 1), second)
            for parity, value in ((0, even), (1, odd)):
                start = (parity * steps + t) * row_blocks
                out_ref[start : start + row_blocks, u * LANES : (u + 1) * LANES] = value
    full = out_ref[...]
    high_ref[...], low_ref[...] = split(full)
    high_t_ref[...], low_t_ref[...] = split(full.T)


def solution(mesh):
    return sharded(mesh)


def sharded(mesh):
    return jax.shard_map(
        layer,
        mesh=mesh,
        in_specs=(
            P(("rep", "row"), None),
            P(),
            P(),
            P(("rep", "row"), None),
            P("rep", "row", None, None),
            P("rep", "row", None),
            P("rep", "row", None),
            P("rep", "row"),
            P("rep", None),
        ),
        out_specs=(P(("rep", "row"), None), P(("rep", "row"), None), P(), P()),
        check_vma=False,
    )
```

```python
import functools

import jax
import jax.numpy as jnp
from jax import lax
from jax.experimental import pallas as pl
from jax.experimental.pallas import tpu as pltpu
from jax.sharding import PartitionSpec as P


BS = 64
LANES = 128
PAD = 8
FLOOR = 16 * 2**20
F32 = jnp.float32
BF16 = jnp.bfloat16
NN = (((1,), (0,)), ((), ()))
TN = (((0,), (0,)), ((), ()))
NT = (((1,), (1,)), ((), ()))


def split(x):
    high = x.astype(BF16)
    return high, (x - high.astype(F32)).astype(BF16)


def mm(a, b, dims):
    return lax.dot_general(a, b, dims, preferred_element_type=F32)


def mm3(a, b, dims):
    return mm(a[0], b[0], dims) + (mm(a[0], b[1], dims) + mm(a[1], b[0], dims))


def call(kernel, outs, args, scratch=(), flops=0, smem=(), hbm=()):
    out_bytes = sum(int(o.size) * o.dtype.itemsize for o in outs)
    in_bytes = sum(int(a.size) * a.dtype.itemsize for a in args)
    limit = max(FLOOR, 4 * (in_bytes + out_bytes))
    return pl.pallas_call(
        kernel,
        out_shape=outs,
        in_specs=[
            pl.BlockSpec(
                memory_space=pltpu.SMEM if k in smem else pltpu.HBM if k in hbm else pltpu.VMEM
            )
            for k in range(len(args))
        ],
        out_specs=[pl.BlockSpec(memory_space=pltpu.VMEM) for _ in outs],
        scratch_shapes=list(scratch),
        cost_estimate=pl.CostEstimate(
            flops=flops, transcendentals=0, bytes_accessed=in_bytes + out_bytes
        ),
        compiler_params=pltpu.CompilerParams(vmem_limit_bytes=limit),
    )(*args)


def rows_at(index, count):
    return pl.ds(pl.multiple_of(index * count, count), count)


def one_hot(wanted, nodes):
    node = lax.broadcasted_iota(jnp.int32, (nodes, wanted.shape[1]), 0)
    return (node == wanted).astype(BF16)


def tree_sum(terms):
    terms = list(terms)
    while len(terms) > 1:
        terms = [terms[k] + terms[k + 1] for k in range(0, len(terms), 2)]
    return terms[0]


def put_pairs(outs, buffer, me, per):
    for pair, out in enumerate(outs):
        for core in range(2):
            source = rows_at(lax.bitwise_xor(me, 2 * pair + core), per)
            out[core * per : (core + 1) * per, :] = buffer[source, :]


def take_pairs(own_ref, partner_ref, buffer, me, per):
    for pair in range(buffer.shape[0] // (2 * per)):
        rows = slice(pair * per, (pair + 1) * per)
        buffer[rows_at(lax.bitwise_xor(me, 2 * pair), per), :] = own_ref[rows, :]
        buffer[rows_at(lax.bitwise_xor(me, 2 * pair + 1), per), :] = partner_ref[rows, :]


def gather_rows(list_hbm, feat_hbm, *refs):
    outs, wanted_ref, feat_ref, buffer, sems = refs[:-4], refs[-4], refs[-3], refs[-2], refs[-1]
    me = lax.axis_index("row")
    slots = buffer.shape[0]
    copies = [
        pltpu.make_async_copy(feat_hbm, feat_ref, sems.at[0]),
        pltpu.make_async_copy(list_hbm.at[:, rows_at(me, slots)], wanted_ref, sems.at[1]),
    ]
    for copy in copies:
        copy.start()
    for copy in copies:
        copy.wait()
    pick = one_hot(wanted_ref[...], feat_ref.shape[0])
    high, low = split(feat_ref[...])
    buffer[...] = mm(pick, high, TN) + mm(pick, low, TN)
    put_pairs(outs, buffer, me, outs[0].shape[0] // 2)


def aggregate(groups, row_blocks, per, high_ref, low_ref, own_ref, partner_ref, *refs):
    outs, border, natural = refs[:groups], refs[groups], refs[groups + 1]
    me, group = lax.axis_index("row"), lax.axis_index("rep")
    take_pairs(own_ref, partner_ref, border, me, per)
    result = mm3((high_ref[...], low_ref[...]), split(border[...]), NN)
    unmix(result, natural, row_blocks)
    nodes = outs[0].shape[0]
    for s in range(groups):
        for part in range(natural.shape[0]):
            outs[s][:, part * LANES : (part + 1) * LANES] = natural[
                part, rows_at(lax.bitwise_xor(group, s), nodes), :
            ]


def unmix(result, natural, row_blocks):
    for m in range(BS):
        start = ((m % 2) * (BS // 2) + m // 2) * row_blocks
        for part in range(natural.shape[0]):
            natural[part, pl.ds(m, row_blocks, stride=BS), :] = result[
                start : start + row_blocks, part * LANES : (part + 1) * LANES
            ]


def activate(groups, members, *refs):
    pieces = refs[:groups]
    weight_ref, bias_ref, cot_ref, act_ref, grad_ref, keep_ref, send_ref, buffer = refs[groups:]
    me = lax.axis_index("row")
    total = tree_sum([piece[...] for piece in pieces])
    total_split = split(total)
    pre = mm3(total_split, split(weight_ref[...]), NN) + bias_ref[...]
    gate = jax.nn.sigmoid(pre)
    act_ref[...] = pre * gate
    grad = cot_ref[...] * (gate * (1.0 + pre * (1.0 - gate)))
    grad_ref[...] = grad
    buffer[...] = mm3(total_split, split(grad), TN)
    chunk = buffer.shape[0] // members
    sums = jnp.broadcast_to(jnp.sum(grad, axis=0, keepdims=True), (PAD, grad.shape[1]))
    for s in range(members):
        target = send_ref if s % 2 else keep_ref
        start = (s // 2) * (chunk + PAD)
        target[start : start + chunk, :] = buffer[rows_at(lax.bitwise_xor(me, s), chunk), :]
        target[start + chunk : start + chunk + PAD, :] = sums


def spread(groups, pairs, row_blocks, high_ref, low_ref, *refs):
    pieces, outs = refs[:groups], refs[groups : groups + pairs]
    natural, border = refs[groups + pairs :]
    me, group = lax.axis_index("row"), lax.axis_index("rep")
    nodes = pieces[0].shape[0]
    for s in range(groups):
        for part in range(natural.shape[0]):
            natural[part, rows_at(lax.bitwise_xor(group, s), nodes), :] = pieces[s][
                :, part * LANES : (part + 1) * LANES
            ]
    order = []
    for parity in range(2):
        for t in range(BS // 2):
            order.append(
                jnp.concatenate(
                    [
                        natural[part, pl.ds(2 * t + parity, row_blocks, stride=BS), :]
                        for part in range(natural.shape[0])
                    ],
                    axis=1,
                )
            )
    mixed = jnp.concatenate(order, axis=0)
    border[...] = mm3((high_ref[...], low_ref[...]), split(mixed), NN)
    put_pairs(outs, border, me, outs[0].shape[0] // 2)


def collect(per, wanted_ref, weight_ref, own_ref, partner_ref, out_ref, border):
    me = lax.axis_index("row")
    take_pairs(own_ref, partner_ref, border, me, per)
    pick = one_hot(wanted_ref[...], out_ref.shape[0])
    high, low = split(border[...])
    proj = mm(pick, high, NN) + mm(pick, low, NN)
    out_ref[...] = mm3(split(proj), split(weight_ref[...]), NT)


def finish(members, summed_ref, own_ref, partner_ref, weight_ref, bias_ref):
    me = lax.axis_index("row")
    chunk = weight_ref.shape[0] // members
    for s in range(members):
        piece = partner_ref if s % 2 else own_ref
        start = (s // 2) * chunk
        weight_ref[rows_at(lax.bitwise_xor(me, s), chunk), :] = piece[start : start + chunk, :]
    bias_ref[...] = summed_ref[chunk : chunk + 1, :]


def exchange(value, axis, shift):
    size = lax.axis_size(axis)
    return lax.ppermute(value, axis, [(i, i ^ shift) for i in range(size)])


def swap_rows(sends):
    pieces = [sends[0]]
    pieces += [exchange(sends[p], "row", 2 * p) for p in range(1, len(sends))]
    per = sends[0].shape[0] // 2
    own = jnp.concatenate([piece[:per] for piece in pieces], axis=0)
    partner = jnp.concatenate([piece[per:] for piece in pieces], axis=0)
    return [own, exchange(partner, "row", 1)]


def layer(
    node_feat, weight, bias, cotangent, blocks, row_block, col_block, live_blocks, send_list
):
    nodes, width = node_feat.shape
    groups, members = lax.axis_size("rep"), lax.axis_size("row")
    capacity = blocks.shape[2]
    per = send_list.shape[-1] // (members * members)
    slots = members * per
    row_blocks = groups * nodes // BS
    col_blocks = slots // BS
    rows = row_blocks * BS
    pairs = members // 2
    shape = lambda n: jax.ShapeDtypeStruct((n, width), F32)
    vmem = lambda n: pltpu.VMEM((n, width), F32)
    tiles = pltpu.VMEM((width // LANES, rows, LANES), F32)

    *sends, wanted = call(
        gather_rows,
        [shape(2 * per)] * pairs + [jax.ShapeDtypeStruct((1, slots), jnp.int32)],
        [pltpu.with_memory_space_constraint(x, pltpu.HBM) for x in (send_list, node_feat)],
        [vmem(nodes), vmem(slots), pltpu.SemaphoreType.DMA((2,))],
        hbm=(0, 1),
    )
    border = swap_rows(sends)
    wide = jax.ShapeDtypeStruct((rows, slots), BF16)
    tall = jax.ShapeDtypeStruct((slots, rows), BF16)
    bias_row = jax.ShapeDtypeStruct((1, width), F32)
    *dense, bias_here = call(
        functools.partial(build, row_blocks, col_blocks),
        [wide, wide, tall, tall, bias_row],
        [live_blocks, row_block[0], col_block[0], blocks[0, 0], bias[None, :]],
        [pltpu.VMEM((rows, slots), F32)],
        flops=4 * row_blocks * col_blocks * capacity * BS * BS,
        smem=(0,),
    )
    partials = call(
        functools.partial(aggregate, groups, row_blocks, per),
        [shape(nodes)] * groups,
        dense[:2] + border,
        [vmem(slots), tiles],
        flops=6 * rows * slots * width,
    )
    parts = [partials[0]] + [exchange(partials[s], "rep", s) for s in range(1, groups)]
    chunk = width // members
    padded = pairs * (chunk + PAD)
    activated, grad, keep, send = call(
        functools.partial(activate, groups, members),
        [shape(nodes), shape(nodes), shape(padded), shape(padded)],
        parts + [weight, bias_here, cotangent],
        [vmem(width)],
        flops=12 * nodes * width * width,
    )
    grads = [grad] + [exchange(grad, "rep", s) for s in range(1, groups)]
    backs = call(
        functools.partial(spread, groups, pairs, row_blocks),
        [shape(2 * per)] * pairs,
        dense[2:] + grads,
        [tiles, vmem(slots)],
        flops=6 * rows * slots * width,
    )
    returned = swap_rows(backs)
    (feat_grad,) = call(
        functools.partial(collect, per),
        [shape(nodes)],
        [wanted, weight] + returned,
        [vmem(slots)],
        flops=6 * nodes * width * width,
    )
    total = keep + exchange(send, "row", 1)
    size = chunk + PAD
    owned = [total[p * size : (p + 1) * size] for p in range(pairs)]
    owned[1:] = [exchange(owned[p], "row", 2 * p) for p in range(1, pairs)]
    part = tree_sum(owned)
    summed = tree_sum([part] + [exchange(part, "rep", s) for s in range(1, groups)])
    done = summed[:chunk]
    chunks = [done] + [exchange(done, "row", 2 * p) for p in range(1, pairs)]
    own = jnp.concatenate(chunks, axis=0)
    partner = exchange(own, "row", 1)
    weight_grad, bias_grad = call(
        functools.partial(finish, members), [shape(width), shape(1)], [summed, own, partner]
    )
    return (activated, feat_grad, weight_grad, bias_grad[0])


def build(row_blocks, col_blocks, live_ref, rows_ref, cols_ref, blocks_ref, bias_ref, *refs):
    high_ref, low_ref, high_t_ref, low_t_ref, bias_out, out_ref = refs
    bias_out[...] = bias_ref[...]
    capacity = blocks_ref.shape[0]
    pairs = row_blocks * col_blocks
    steps = blocks_ref.shape[1] // LANES
    pair_of = cols_ref[...] * row_blocks + rows_ref[...]
    pair = lax.broadcasted_iota(jnp.int32, (pairs, capacity), 0)
    slot = lax.broadcasted_iota(jnp.int32, (pairs, capacity), 1)
    pick = ((pair == pair_of) & (slot < live_ref[0, 0])).astype(BF16)
    high, low = split(blocks_ref[...])
    dense = mm(pick, high, NN) + mm(pick, low, NN)
    left = lax.broadcasted_iota(jnp.int32, (row_blocks, LANES), 1) < BS
    for t in range(steps):
        lanes = slice(t * LANES, (t + 1) * LANES)
        for u in range(col_blocks // 2):
            first = dense[2 * u * row_blocks : (2 * u + 1) * row_blocks, lanes]
            second = dense[(2 * u + 1) * row_blocks : (2 * u + 2) * row_blocks, lanes]
            even = jnp.where(left, first, pltpu.roll(second, BS, 1))
            odd = jnp.where(left, pltpu.roll(first, BS, 1), second)
            for parity, value in ((0, even), (1, odd)):
                start = (parity * steps + t) * row_blocks
                out_ref[start : start + row_blocks, u * LANES : (u + 1) * LANES] = value
    full = out_ref[...]
    high_ref[...], low_ref[...] = split(full)
    high_t_ref[...], low_t_ref[...] = split(full.T)


def solution(mesh):
    return sharded(mesh)


def sharded(mesh):
    return jax.shard_map(
        layer,
        mesh=mesh,
        in_specs=(
            P(("rep", "row"), None),
            P(),
            P(),
            P(("rep", "row"), None),
            P("rep", "row", None, None),
            P("rep", "row", None),
            P("rep", "row", None),
            P("rep", "row"),
            P("rep", None),
        ),
        out_specs=(P(("rep", "row"), None), P(("rep", "row"), None), P(), P()),
        check_vma=False,
    )
```

```python
import functools

import jax
import jax.numpy as jnp
from jax import lax
from jax.experimental import pallas as pl
from jax.experimental.pallas import tpu as pltpu
from jax.sharding import PartitionSpec as P


BS = 64
LANES = 128
PAD = 8
FLOOR = 16 * 2**20
F32 = jnp.float32
BF16 = jnp.bfloat16
NN = (((1,), (0,)), ((), ()))
TN = (((0,), (0,)), ((), ()))
NT = (((1,), (1,)), ((), ()))


def split(x):
    high = x.astype(BF16)
    return high, (x - high.astype(F32)).astype(BF16)


def mm(a, b, dims):
    return lax.dot_general(a, b, dims, preferred_element_type=F32)


def mm3(a, b, dims):
    return mm(a[0], b[0], dims) + (mm(a[0], b[1], dims) + mm(a[1], b[0], dims))


def call(kernel, outs, args, scratch=(), flops=0, smem=(), hbm=(), hbm_out=()):
    out_bytes = sum(int(o.size) * o.dtype.itemsize for o in outs)
    in_bytes = sum(int(a.size) * a.dtype.itemsize for a in args)
    limit = max(FLOOR, 4 * (in_bytes + out_bytes))
    return pl.pallas_call(
        kernel,
        out_shape=outs,
        in_specs=[
            pl.BlockSpec(
                memory_space=pltpu.SMEM if k in smem else pltpu.HBM if k in hbm else pltpu.VMEM
            )
            for k in range(len(args))
        ],
        out_specs=[
            pl.BlockSpec(memory_space=pltpu.HBM if k in hbm_out else pltpu.VMEM)
            for k in range(len(outs))
        ],
        scratch_shapes=list(scratch),
        cost_estimate=pl.CostEstimate(
            flops=flops, transcendentals=0, bytes_accessed=in_bytes + out_bytes
        ),
        compiler_params=pltpu.CompilerParams(vmem_limit_bytes=limit),
    )(*args)


def rows_at(index, count):
    return pl.ds(pl.multiple_of(index * count, count), count)


def one_hot(wanted, nodes):
    node = lax.broadcasted_iota(jnp.int32, (nodes, wanted.shape[1]), 0)
    return (node == wanted).astype(BF16)


def tree_sum(terms):
    terms = list(terms)
    while len(terms) > 1:
        terms = [terms[k] + terms[k + 1] for k in range(0, len(terms), 2)]
    return terms[0]


def put_pairs(outs, buffer, me, per):
    for pair, out in enumerate(outs):
        for core in range(2):
            source = rows_at(lax.bitwise_xor(me, 2 * pair + core), per)
            out[core * per : (core + 1) * per, :] = buffer[source, :]


def take_pairs(own_ref, partner_ref, buffer, me, per):
    for pair in range(buffer.shape[0] // (2 * per)):
        rows = slice(pair * per, (pair + 1) * per)
        buffer[rows_at(lax.bitwise_xor(me, 2 * pair), per), :] = own_ref[rows, :]
        buffer[rows_at(lax.bitwise_xor(me, 2 * pair + 1), per), :] = partner_ref[rows, :]


def gather_rows(list_hbm, feat_hbm, *refs):
    outs, wanted_ref, feat_ref, buffer, sems = refs[:-4], refs[-4], refs[-3], refs[-2], refs[-1]
    me = lax.axis_index("row")
    slots = buffer.shape[0]
    copies = [
        pltpu.make_async_copy(feat_hbm, feat_ref, sems.at[0]),
        pltpu.make_async_copy(list_hbm.at[:, rows_at(me, slots)], wanted_ref, sems.at[1]),
    ]
    for copy in copies:
        copy.start()
    for copy in copies:
        copy.wait()
    pick = one_hot(wanted_ref[...], feat_ref.shape[0])
    high, low = split(feat_ref[...])
    buffer[...] = mm(pick, high, TN) + mm(pick, low, TN)
    put_pairs(outs, buffer, me, outs[0].shape[0] // 2)


def aggregate(pairs, high_ref, low_ref, own_ref, partner_ref, *outs):
    per = own_ref.shape[0] // pairs
    pieces = []
    for pair in range(pairs):
        for ref in (own_ref, partner_ref):
            pieces.append(ref[pair * per : (pair + 1) * per, :])
    border = jnp.concatenate(pieces, axis=0)
    result = mm3((high_ref[...], low_ref[...]), split(border), NN)
    for s, out in enumerate(outs):
        out[...] = result[s * out.shape[0] : (s + 1) * out.shape[0], :]


def activate(groups, members, *refs):
    pieces = refs[:groups]
    high_ref, low_ref, bias_ref, cot_ref, act_ref, grad_ref, keep_ref, send_ref, buffer = refs[groups:]
    me = lax.axis_index("row")
    total = tree_sum([piece[...] for piece in pieces])
    total_split = split(total)
    pre = mm3(total_split, (high_ref[...], low_ref[...]), NN) + bias_ref[...]
    gate = jax.nn.sigmoid(pre)
    act_ref[...] = pre * gate
    grad = cot_ref[...] * (gate * (1.0 + pre * (1.0 - gate)))
    grad_ref[...] = grad
    buffer[...] = mm3(total_split, split(grad), TN)
    chunk = buffer.shape[0] // members
    sums = jnp.broadcast_to(jnp.sum(grad, axis=0, keepdims=True), (PAD, grad.shape[1]))
    for s in range(members):
        target = send_ref if s % 2 else keep_ref
        start = (s // 2) * (chunk + PAD)
        target[start : start + chunk, :] = buffer[rows_at(lax.bitwise_xor(me, s), chunk), :]
        target[start + chunk : start + chunk + PAD, :] = sums


def spread(groups, high_ref, low_ref, *refs):
    pieces, outs = refs[:groups], refs[groups:]
    grads = jnp.concatenate([piece[...] for piece in pieces], axis=0)
    result = mm3((high_ref[...], low_ref[...]), split(grads), NN)
    for pair, out in enumerate(outs):
        out[...] = result[pair * out.shape[0] : (pair + 1) * out.shape[0], :]


def collect(per, wanted_ref, high_ref, low_ref, own_ref, partner_ref, out_ref, border):
    me = lax.axis_index("row")
    take_pairs(own_ref, partner_ref, border, me, per)
    pick = one_hot(wanted_ref[...], out_ref.shape[0])
    high, low = split(border[...])
    proj = mm(pick, high, NN) + mm(pick, low, NN)
    out_ref[...] = mm3(split(proj), (high_ref[...], low_ref[...]), NT)


def finish(members, summed_ref, own_ref, partner_ref, weight_hbm, bias_ref, sems):
    me = lax.axis_index("row")
    chunk = weight_hbm.shape[0] // members
    copies = []
    for s in range(members):
        piece = partner_ref if s % 2 else own_ref
        source = piece.at[(s // 2) * chunk : (s // 2 + 1) * chunk, :]
        target = weight_hbm.at[rows_at(lax.bitwise_xor(me, s), chunk), :]
        copies.append(pltpu.make_async_copy(source, target, sems.at[s]))
    for copy in copies:
        copy.start()
    bias_ref[...] = summed_ref[chunk : chunk + 1, :]
    for copy in copies:
        copy.wait()


def exchange(value, axis, shift):
    size = lax.axis_size(axis)
    return lax.ppermute(value, axis, [(i, i ^ shift) for i in range(size)])


def swap_rows(sends):
    pieces = [sends[0]]
    pieces += [exchange(sends[p], "row", 2 * p) for p in range(1, len(sends))]
    per = sends[0].shape[0] // 2
    own = jnp.concatenate([piece[:per] for piece in pieces], axis=0)
    partner = jnp.concatenate([piece[per:] for piece in pieces], axis=0)
    return [own, exchange(partner, "row", 1)]


def layer(
    node_feat, weight, bias, cotangent, blocks, row_block, col_block, live_blocks, send_list
):
    nodes, width = node_feat.shape
    groups, members = lax.axis_size("rep"), lax.axis_size("row")
    capacity = blocks.shape[2]
    per = send_list.shape[-1] // (members * members)
    slots = members * per
    row_blocks = groups * nodes // BS
    col_blocks = slots // BS
    rows = row_blocks * BS
    assert 2 * per == BS and nodes % BS == 0
    pairs = members // 2
    shape = lambda n: jax.ShapeDtypeStruct((n, width), F32)
    vmem = lambda n: pltpu.VMEM((n, width), F32)

    *sends, wanted = call(
        gather_rows,
        [shape(2 * per)] * pairs + [jax.ShapeDtypeStruct((1, slots), jnp.int32)],
        [pltpu.with_memory_space_constraint(x, pltpu.HBM) for x in (send_list, node_feat)],
        [vmem(nodes), vmem(slots), pltpu.SemaphoreType.DMA((2,))],
        hbm=(0, 1),
    )
    border = swap_rows(sends)
    wide = jax.ShapeDtypeStruct((rows, slots), BF16)
    tall = jax.ShapeDtypeStruct((slots, rows), BF16)
    bias_row = jax.ShapeDtypeStruct((1, width), F32)
    half_weight = jax.ShapeDtypeStruct(weight.shape, BF16)
    *dense, bias_here, weight_high, weight_low = call(
        functools.partial(build, nodes // BS),
        [wide, wide, tall, tall, bias_row, half_weight, half_weight],
        [live_blocks, row_block[0], col_block[0], blocks[0, 0], bias[None, :], weight],
        [pltpu.VMEM((slots // LANES, rows, LANES), F32)],
        flops=4 * row_blocks * col_blocks * capacity * BS * BS,
        smem=(0,),
    )
    partials = call(
        functools.partial(aggregate, pairs),
        [shape(nodes)] * groups,
        dense[:2] + border,
        flops=6 * rows * slots * width,
    )
    parts = [partials[0]] + [exchange(partials[s], "rep", s) for s in range(1, groups)]
    chunk = width // members
    padded = pairs * (chunk + PAD)
    activated, grad, keep, send = call(
        functools.partial(activate, groups, members),
        [shape(nodes), shape(nodes), shape(padded), shape(padded)],
        parts + [weight_high, weight_low, bias_here, cotangent],
        [vmem(width)],
        flops=12 * nodes * width * width,
    )
    grads = [grad] + [exchange(grad, "rep", s) for s in range(1, groups)]
    backs = call(
        functools.partial(spread, groups),
        [shape(2 * per)] * pairs,
        dense[2:] + grads,
        flops=6 * rows * slots * width,
    )
    returned = swap_rows(backs)
    (feat_grad,) = call(
        functools.partial(collect, per),
        [shape(nodes)],
        [wanted, weight_high, weight_low] + returned,
        [vmem(slots)],
        flops=6 * nodes * width * width,
    )
    total = keep + exchange(send, "row", 1)
    size = chunk + PAD
    owned = [total[p * size : (p + 1) * size] for p in range(pairs)]
    owned[1:] = [exchange(owned[p], "row", 2 * p) for p in range(1, pairs)]
    part = tree_sum(owned)
    summed = tree_sum([part] + [exchange(part, "rep", s) for s in range(1, groups)])
    done = summed[:chunk]
    chunks = [done] + [exchange(done, "row", 2 * p) for p in range(1, pairs)]
    own = jnp.concatenate(chunks, axis=0)
    partner = exchange(own, "row", 1)
    weight_grad, bias_grad = call(
        functools.partial(finish, members),
        [shape(width), shape(1)],
        [summed, own, partner],
        [pltpu.SemaphoreType.DMA((members,))],
        hbm_out=(0,),
    )
    return (activated, feat_grad, weight_grad, bias_grad[0])


def build(shard_blocks, live_ref, rows_ref, cols_ref, blocks_ref, bias_ref, weight_ref, *refs):
    high_ref, low_ref, high_t_ref, low_t_ref, bias_out, weight_high, weight_low, dense = refs
    bias_out[...] = bias_ref[...]
    weight_high[...], weight_low[...] = split(weight_ref[...])
    row_blocks = high_ref.shape[0] // BS
    col_blocks = high_ref.shape[1] // BS
    capacity = blocks_ref.shape[0]
    pairs = row_blocks * col_blocks
    me, group = lax.axis_index("row"), lax.axis_index("rep")
    rows = lax.bitwise_xor(rows_ref[...], group * shard_blocks)
    cols = lax.bitwise_xor(cols_ref[...], me // 2)
    pair = lax.broadcasted_iota(jnp.int32, (pairs, capacity), 0)
    slot = lax.broadcasted_iota(jnp.int32, (pairs, capacity), 1)
    pick = ((pair == cols * row_blocks + rows) & (slot < live_ref[0, 0])).astype(BF16)
    high, low = split(blocks_ref[...])
    product = mm(pick, high, NN) + mm(pick, low, NN)
    lane = lax.broadcasted_iota(jnp.int32, (row_blocks, LANES), 1)
    left = lane < BS
    upper = lane % BS < BS // 2
    same = me % 2 == 0
    for t in range(blocks_ref.shape[1] // LANES):
        lanes = slice(t * LANES, (t + 1) * LANES)
        for u in range(col_blocks // 2):
            first = product[2 * u * row_blocks : (2 * u + 1) * row_blocks, lanes]
            second = product[(2 * u + 1) * row_blocks : (2 * u + 2) * row_blocks, lanes]
            even = jnp.where(left, first, pltpu.roll(second, BS, 1))
            odd = jnp.where(left, pltpu.roll(first, BS, 1), second)
            for parity, value in ((0, even), (1, odd)):
                swapped = jnp.where(
                    upper, pltpu.roll(value, LANES - BS // 2, 1), pltpu.roll(value, BS // 2, 1)
                )
                value = jnp.where(same, value, swapped)
                dense[u, pl.ds(2 * t + parity, row_blocks, stride=BS), :] = value
    full = jnp.concatenate([dense[u] for u in range(col_blocks // 2)], axis=1)
    high_ref[...], low_ref[...] = split(full)
    high_t_ref[...], low_t_ref[...] = split(full.T)


def solution(mesh):
    return sharded(mesh)


def sharded(mesh):
    return jax.shard_map(
        layer,
        mesh=mesh,
        in_specs=(
            P(("rep", "row"), None),
            P(),
            P(),
            P(("rep", "row"), None),
            P("rep", "row", None, None),
            P("rep", "row", None),
            P("rep", "row", None),
            P("rep", "row"),
            P("rep", None),
        ),
        out_specs=(P(("rep", "row"), None), P(("rep", "row"), None), P(), P()),
        check_vma=False,
    )
```

```python
import functools

import jax
import jax.numpy as jnp
from jax import lax
from jax.experimental import pallas as pl
from jax.experimental.pallas import tpu as pltpu
from jax.sharding import PartitionSpec as P


BS = 64
LANES = 128
PAD = 8
FLOOR = 16 * 2**20
F32 = jnp.float32
BF16 = jnp.bfloat16
NN = (((1,), (0,)), ((), ()))
TN = (((0,), (0,)), ((), ()))
NT = (((1,), (1,)), ((), ()))


def split(x):
    high = x.astype(BF16)
    return high, (x - high.astype(F32)).astype(BF16)


def mm(a, b, dims):
    return lax.dot_general(a, b, dims, preferred_element_type=F32)


def mm3(a, b, dims):
    return mm(a[0], b[0], dims) + (mm(a[0], b[1], dims) + mm(a[1], b[0], dims))


def call(kernel, outs, args, scratch=(), flops=0, smem=(), hbm=()):
    out_bytes = sum(int(o.size) * o.dtype.itemsize for o in outs)
    in_bytes = sum(int(a.size) * a.dtype.itemsize for a in args)
    limit = max(FLOOR, 4 * (in_bytes + out_bytes))
    return pl.pallas_call(
        kernel,
        out_shape=outs,
        in_specs=[
            pl.BlockSpec(
                memory_space=pltpu.SMEM if k in smem else pltpu.HBM if k in hbm else pltpu.VMEM
            )
            for k in range(len(args))
        ],
        out_specs=[pl.BlockSpec(memory_space=pltpu.VMEM) for _ in outs],
        scratch_shapes=list(scratch),
        cost_estimate=pl.CostEstimate(
            flops=flops, transcendentals=0, bytes_accessed=in_bytes + out_bytes
        ),
        compiler_params=pltpu.CompilerParams(vmem_limit_bytes=limit),
    )(*args)


def rows_at(index, count):
    return pl.ds(pl.multiple_of(index * count, count), count)


def one_hot(wanted, nodes):
    node = lax.broadcasted_iota(jnp.int32, (nodes, wanted.shape[1]), 0)
    return (node == wanted).astype(BF16)


def tree_sum(terms):
    terms = list(terms)
    while len(terms) > 1:
        terms = [terms[k] + terms[k + 1] for k in range(0, len(terms), 2)]
    return terms[0]


def put_pairs(outs, buffer, me, per):
    for pair, out in enumerate(outs):
        for core in range(2):
            source = rows_at(lax.bitwise_xor(me, 2 * pair + core), per)
            out[core * per : (core + 1) * per, :] = buffer[source, :]


def take_pairs(own_ref, partner_ref, buffer, me, per):
    for pair in range(buffer.shape[0] // (2 * per)):
        rows = slice(pair * per, (pair + 1) * per)
        buffer[rows_at(lax.bitwise_xor(me, 2 * pair), per), :] = own_ref[rows, :]
        buffer[rows_at(lax.bitwise_xor(me, 2 * pair + 1), per), :] = partner_ref[rows, :]


def gather_rows(list_hbm, feat_hbm, *refs):
    outs, wanted_ref, feat_ref, buffer, sems = refs[:-4], refs[-4], refs[-3], refs[-2], refs[-1]
    me = lax.axis_index("row")
    slots = buffer.shape[0]
    copies = [
        pltpu.make_async_copy(feat_hbm, feat_ref, sems.at[0]),
        pltpu.make_async_copy(list_hbm.at[:, rows_at(me, slots)], wanted_ref, sems.at[1]),
    ]
    for copy in copies:
        copy.start()
    for copy in copies:
        copy.wait()
    pick = one_hot(wanted_ref[...], feat_ref.shape[0])
    high, low = split(feat_ref[...])
    buffer[...] = mm(pick, high, TN) + mm(pick, low, TN)
    put_pairs(outs, buffer, me, outs[0].shape[0] // 2)


def aggregate(pairs, high_ref, low_ref, own_ref, partner_ref, *outs):
    per = own_ref.shape[0] // pairs
    pieces = []
    for pair in range(pairs):
        for ref in (own_ref, partner_ref):
            pieces.append(ref[pair * per : (pair + 1) * per, :])
    border = jnp.concatenate(pieces, axis=0)
    result = mm3((high_ref[...], low_ref[...]), split(border), NN)
    for s, out in enumerate(outs):
        out[...] = result[s * out.shape[0] : (s + 1) * out.shape[0], :]


def activate(groups, members, *refs):
    pieces = refs[:groups]
    high_ref, low_ref, bias_ref, cot_ref, pre_ref, grad_ref, keep_ref, send_ref, buffer = refs[groups:]
    me = lax.axis_index("row")
    total = tree_sum([piece[...] for piece in pieces])
    total_split = split(total)
    pre = mm3(total_split, (high_ref[...], low_ref[...]), NN) + bias_ref[...]
    gate = jax.nn.sigmoid(pre)
    pre_ref[...] = pre
    grad = cot_ref[...] * (gate * (1.0 + pre * (1.0 - gate)))
    grad_ref[...] = grad
    buffer[...] = mm3(total_split, split(grad), TN)
    chunk = buffer.shape[0] // members
    sums = jnp.broadcast_to(jnp.sum(grad, axis=0, keepdims=True), (PAD, grad.shape[1]))
    for s in range(members):
        target = send_ref if s % 2 else keep_ref
        start = (s // 2) * (chunk + PAD)
        target[start : start + chunk, :] = buffer[rows_at(lax.bitwise_xor(me, s), chunk), :]
        target[start + chunk : start + chunk + PAD, :] = sums


def spread(groups, high_ref, low_ref, *refs):
    pieces, outs = refs[:groups], refs[groups:]
    grads = jnp.concatenate([piece[...] for piece in pieces], axis=0)
    result = mm3((high_ref[...], low_ref[...]), split(grads), NN)
    for pair, out in enumerate(outs):
        out[...] = result[pair * out.shape[0] : (pair + 1) * out.shape[0], :]


def collect(per, wanted_ref, high_ref, low_ref, own_ref, partner_ref, out_ref, border):
    me = lax.axis_index("row")
    take_pairs(own_ref, partner_ref, border, me, per)
    pick = one_hot(wanted_ref[...], out_ref.shape[0])
    high, low = split(border[...])
    proj = mm(pick, high, NN) + mm(pick, low, NN)
    out_ref[...] = mm3(split(proj), (high_ref[...], low_ref[...]), NT)


def finish(members, summed_ref, own_ref, partner_ref, weight_ref, bias_ref):
    me = lax.axis_index("row")
    chunk = weight_ref.shape[0] // members
    for s in range(members):
        piece = partner_ref if s % 2 else own_ref
        start = (s // 2) * chunk
        weight_ref[rows_at(lax.bitwise_xor(me, s), chunk), :] = piece[start : start + chunk, :]
    bias_ref[...] = summed_ref[chunk : chunk + 1, :]


def emit(pre_ref, act_ref):
    pre = pre_ref[...]
    act_ref[...] = pre * jax.nn.sigmoid(pre)


def exchange(value, axis, shift):
    size = lax.axis_size(axis)
    return lax.ppermute(value, axis, [(i, i ^ shift) for i in range(size)])


def swap_rows(sends):
    pieces = [sends[0]]
    pieces += [exchange(sends[p], "row", 2 * p) for p in range(1, len(sends))]
    per = sends[0].shape[0] // 2
    own = jnp.concatenate([piece[:per] for piece in pieces], axis=0)
    partner = jnp.concatenate([piece[per:] for piece in pieces], axis=0)
    return [own, exchange(partner, "row", 1)]


def layer(
    node_feat, weight, bias, cotangent, blocks, row_block, col_block, live_blocks, send_list
):
    nodes, width = node_feat.shape
    groups, members = lax.axis_size("rep"), lax.axis_size("row")
    capacity = blocks.shape[2]
    per = send_list.shape[-1] // (members * members)
    slots = members * per
    row_blocks = groups * nodes // BS
    col_blocks = slots // BS
    rows = row_blocks * BS
    assert 2 * per == BS and nodes % BS == 0
    pairs = members // 2
    shape = lambda n: jax.ShapeDtypeStruct((n, width), F32)
    vmem = lambda n: pltpu.VMEM((n, width), F32)

    *sends, wanted = call(
        gather_rows,
        [shape(2 * per)] * pairs + [jax.ShapeDtypeStruct((1, slots), jnp.int32)],
        [pltpu.with_memory_space_constraint(x, pltpu.HBM) for x in (send_list, node_feat)],
        [vmem(nodes), vmem(slots), pltpu.SemaphoreType.DMA((2,))],
        hbm=(0, 1),
    )
    border = swap_rows(sends)
    wide = jax.ShapeDtypeStruct((rows, slots), BF16)
    tall = jax.ShapeDtypeStruct((slots, rows), BF16)
    bias_row = jax.ShapeDtypeStruct((1, width), F32)
    half_weight = jax.ShapeDtypeStruct(weight.shape, BF16)
    *dense, bias_here, weight_high, weight_low = call(
        functools.partial(build, nodes // BS),
        [wide, wide, tall, tall, bias_row, half_weight, half_weight],
        [live_blocks, row_block[0], col_block[0], blocks[0, 0], bias[None, :], weight],
        [pltpu.VMEM((slots // LANES, rows, LANES), F32)],
        flops=4 * row_blocks * col_blocks * capacity * BS * BS,
        smem=(0,),
    )
    partials = call(
        functools.partial(aggregate, pairs),
        [shape(nodes)] * groups,
        dense[:2] + border,
        flops=6 * rows * slots * width,
    )
    parts = [partials[0]] + [exchange(partials[s], "rep", s) for s in range(1, groups)]
    chunk = width // members
    padded = pairs * (chunk + PAD)
    pre, grad, keep, send = call(
        functools.partial(activate, groups, members),
        [shape(nodes), shape(nodes), shape(padded), shape(padded)],
        parts + [weight_high, weight_low, bias_here, cotangent],
        [vmem(width)],
        flops=12 * nodes * width * width,
    )
    (activated,) = call(emit, [shape(nodes)], [pre])
    grads = [grad] + [exchange(grad, "rep", s) for s in range(1, groups)]
    backs = call(
        functools.partial(spread, groups),
        [shape(2 * per)] * pairs,
        dense[2:] + grads,
        flops=6 * rows * slots * width,
    )
    returned = swap_rows(backs)
    (feat_grad,) = call(
        functools.partial(collect, per),
        [shape(nodes)],
        [wanted, weight_high, weight_low] + returned,
        [vmem(slots)],
        flops=6 * nodes * width * width,
    )
    total = keep + exchange(send, "row", 1)
    size = chunk + PAD
    owned = [total[p * size : (p + 1) * size] for p in range(pairs)]
    owned[1:] = [exchange(owned[p], "row", 2 * p) for p in range(1, pairs)]
    part = tree_sum(owned)
    summed = tree_sum([part] + [exchange(part, "rep", s) for s in range(1, groups)])
    done = summed[:chunk]
    chunks = [done] + [exchange(done, "row", 2 * p) for p in range(1, pairs)]
    own = jnp.concatenate(chunks, axis=0)
    partner = exchange(own, "row", 1)
    weight_grad, bias_grad = call(
        functools.partial(finish, members),
        [shape(width), shape(1)],
        [summed, own, partner],
    )
    return (activated, feat_grad, weight_grad, bias_grad[0])


def build(shard_blocks, live_ref, rows_ref, cols_ref, blocks_ref, bias_ref, weight_ref, *refs):
    high_ref, low_ref, high_t_ref, low_t_ref, bias_out, weight_high, weight_low, dense = refs
    bias_out[...] = bias_ref[...]
    weight_high[...], weight_low[...] = split(weight_ref[...])
    row_blocks = high_ref.shape[0] // BS
    col_blocks = high_ref.shape[1] // BS
    capacity = blocks_ref.shape[0]
    pairs = row_blocks * col_blocks
    me, group = lax.axis_index("row"), lax.axis_index("rep")
    rows = lax.bitwise_xor(rows_ref[...], group * shard_blocks)
    cols = lax.bitwise_xor(cols_ref[...], me // 2)
    pair = lax.broadcasted_iota(jnp.int32, (pairs, capacity), 0)
    slot = lax.broadcasted_iota(jnp.int32, (pairs, capacity), 1)
    pick = ((pair == cols * row_blocks + rows) & (slot < live_ref[0, 0])).astype(BF16)
    high, low = split(blocks_ref[...])
    product = mm(pick, high, NN) + mm(pick, low, NN)
    lane = lax.broadcasted_iota(jnp.int32, (row_blocks, LANES), 1)
    left = lane < BS
    upper = lane % BS < BS // 2
    same = me % 2 == 0
    for t in range(blocks_ref.shape[1] // LANES):
        lanes = slice(t * LANES, (t + 1) * LANES)
        for u in range(col_blocks // 2):
            first = product[2 * u * row_blocks : (2 * u + 1) * row_blocks, lanes]
            second = product[(2 * u + 1) * row_blocks : (2 * u + 2) * row_blocks, lanes]
            even = jnp.where(left, first, pltpu.roll(second, BS, 1))
            odd = jnp.where(left, pltpu.roll(first, BS, 1), second)
            for parity, value in ((0, even), (1, odd)):
                swapped = jnp.where(
                    upper, pltpu.roll(value, LANES - BS // 2, 1), pltpu.roll(value, BS // 2, 1)
                )
                value = jnp.where(same, value, swapped)
                dense[u, pl.ds(2 * t + parity, row_blocks, stride=BS), :] = value
    full = jnp.concatenate([dense[u] for u in range(col_blocks // 2)], axis=1)
    high_ref[...], low_ref[...] = split(full)
    high_t_ref[...], low_t_ref[...] = split(full.T)


def solution(mesh):
    return sharded(mesh)


def sharded(mesh):
    return jax.shard_map(
        layer,
        mesh=mesh,
        in_specs=(
            P(("rep", "row"), None),
            P(),
            P(),
            P(("rep", "row"), None),
            P("rep", "row", None, None),
            P("rep", "row", None),
            P("rep", "row", None),
            P("rep", "row"),
            P("rep", None),
        ),
        out_specs=(P(("rep", "row"), None), P(("rep", "row"), None), P(), P()),
        check_vma=False,
    )
```

```python
import functools

import jax
import jax.numpy as jnp
from jax import lax
from jax.experimental import pallas as pl
from jax.experimental.pallas import tpu as pltpu
from jax.sharding import PartitionSpec as P


BS = 64
LANES = 128
PAD = 8
FLOOR = 16 * 2**20
F32 = jnp.float32
BF16 = jnp.bfloat16
NN = (((1,), (0,)), ((), ()))
TN = (((0,), (0,)), ((), ()))
NT = (((1,), (1,)), ((), ()))


def split(x):
    high = x.astype(BF16)
    return high, (x - high.astype(F32)).astype(BF16)


def mm(a, b, dims):
    return lax.dot_general(a, b, dims, preferred_element_type=F32)


def mm3(a, b, dims):
    return mm(a[0], b[0], dims) + (mm(a[0], b[1], dims) + mm(a[1], b[0], dims))


def call(kernel, outs, args, scratch=(), flops=0, smem=(), hbm=()):
    out_bytes = sum(int(o.size) * o.dtype.itemsize for o in outs)
    in_bytes = sum(int(a.size) * a.dtype.itemsize for a in args)
    limit = max(FLOOR, 4 * (in_bytes + out_bytes))
    return pl.pallas_call(
        kernel,
        out_shape=outs,
        in_specs=[
            pl.BlockSpec(
                memory_space=pltpu.SMEM if k in smem else pltpu.HBM if k in hbm else pltpu.VMEM
            )
            for k in range(len(args))
        ],
        out_specs=[pl.BlockSpec(memory_space=pltpu.VMEM) for _ in outs],
        scratch_shapes=list(scratch),
        cost_estimate=pl.CostEstimate(
            flops=flops, transcendentals=0, bytes_accessed=in_bytes + out_bytes
        ),
        compiler_params=pltpu.CompilerParams(vmem_limit_bytes=limit),
    )(*args)


def rows_at(index, count):
    return pl.ds(pl.multiple_of(index * count, count), count)


def one_hot(wanted, nodes):
    node = lax.broadcasted_iota(jnp.int32, (nodes, wanted.shape[1]), 0)
    return (node == wanted).astype(BF16)


def tree_sum(terms):
    terms = list(terms)
    while len(terms) > 1:
        terms = [terms[k] + terms[k + 1] for k in range(0, len(terms), 2)]
    return terms[0]


def put_pairs(outs, buffer, me, per):
    for pair, out in enumerate(outs):
        for core in range(2):
            source = rows_at(lax.bitwise_xor(me, 2 * pair + core), per)
            out[core * per : (core + 1) * per, :] = buffer[source, :]


def take_pairs(own_ref, partner_ref, buffer, me, per):
    for pair in range(buffer.shape[0] // (2 * per)):
        rows = slice(pair * per, (pair + 1) * per)
        buffer[rows_at(lax.bitwise_xor(me, 2 * pair), per), :] = own_ref[rows, :]
        buffer[rows_at(lax.bitwise_xor(me, 2 * pair + 1), per), :] = partner_ref[rows, :]


def gather_rows(list_hbm, feat_hbm, *refs):
    outs, wanted_ref, feat_ref, buffer, sems = refs[:-4], refs[-4], refs[-3], refs[-2], refs[-1]
    me = lax.axis_index("row")
    slots = buffer.shape[0]
    copies = [
        pltpu.make_async_copy(feat_hbm, feat_ref, sems.at[0]),
        pltpu.make_async_copy(list_hbm.at[:, rows_at(me, slots)], wanted_ref, sems.at[1]),
    ]
    for copy in copies:
        copy.start()
    copies[1].wait()
    pick = one_hot(wanted_ref[...], feat_ref.shape[0]).T
    copies[0].wait()
    high, low = split(feat_ref[...])
    buffer[...] = mm(pick, high, NN) + mm(pick, low, NN)
    put_pairs(outs, buffer, me, outs[0].shape[0] // 2)


def aggregate(pairs, high_ref, low_ref, own_ref, partner_ref, *outs):
    per = own_ref.shape[0] // pairs
    pieces = []
    for pair in range(pairs):
        for ref in (own_ref, partner_ref):
            pieces.append(ref[pair * per : (pair + 1) * per, :])
    border = jnp.concatenate(pieces, axis=0)
    result = mm3((high_ref[...], low_ref[...]), split(border), NN)
    for s, out in enumerate(outs):
        out[...] = result[s * out.shape[0] : (s + 1) * out.shape[0], :]


def activate(groups, members, *refs):
    pieces = refs[:groups]
    high_ref, low_ref, bias_ref, cot_ref, pre_ref, grad_ref, keep_ref, send_ref, buffer = refs[groups:]
    me = lax.axis_index("row")
    total = tree_sum([piece[...] for piece in pieces])
    total_split = split(total)
    pre = mm3(total_split, (high_ref[...], low_ref[...]), NN) + bias_ref[...]
    gate = jax.nn.sigmoid(pre)
    pre_ref[...] = pre
    grad = cot_ref[...] * (gate * (1.0 + pre * (1.0 - gate)))
    grad_ref[...] = grad
    buffer[...] = mm3(total_split, split(grad), TN)
    chunk = buffer.shape[0] // members
    sums = jnp.broadcast_to(jnp.sum(grad, axis=0, keepdims=True), (PAD, grad.shape[1]))
    for s in range(members):
        target = send_ref if s % 2 else keep_ref
        start = (s // 2) * (chunk + PAD)
        target[start : start + chunk, :] = buffer[rows_at(lax.bitwise_xor(me, s), chunk), :]
        target[start + chunk : start + chunk + PAD, :] = sums


def spread(groups, high_ref, low_ref, *refs):
    pieces, outs = refs[:groups], refs[groups:]
    grads = jnp.concatenate([piece[...] for piece in pieces], axis=0)
    result = mm3((high_ref[...], low_ref[...]), split(grads), NN)
    for pair, out in enumerate(outs):
        out[...] = result[pair * out.shape[0] : (pair + 1) * out.shape[0], :]


def collect(per, wanted_ref, high_ref, low_ref, own_ref, partner_ref, out_ref, border):
    me = lax.axis_index("row")
    take_pairs(own_ref, partner_ref, border, me, per)
    pick = one_hot(wanted_ref[...], out_ref.shape[0])
    high, low = split(border[...])
    proj = mm(pick, high, NN) + mm(pick, low, NN)
    out_ref[...] = mm3(split(proj), (high_ref[...], low_ref[...]), NT)


def finish(members, summed_ref, own_ref, partner_ref, weight_ref, bias_ref):
    me = lax.axis_index("row")
    chunk = weight_ref.shape[0] // members
    for s in range(members):
        piece = partner_ref if s % 2 else own_ref
        start = (s // 2) * chunk
        weight_ref[rows_at(lax.bitwise_xor(me, s), chunk), :] = piece[start : start + chunk, :]
    bias_ref[...] = summed_ref[chunk : chunk + 1, :]


def emit(pre_ref, act_ref):
    pre = pre_ref[...]
    act_ref[...] = pre * jax.nn.sigmoid(pre)


def exchange(value, axis, shift):
    size = lax.axis_size(axis)
    return lax.ppermute(value, axis, [(i, i ^ shift) for i in range(size)])


def swap_rows(sends):
    pieces = [sends[0]]
    pieces += [exchange(sends[p], "row", 2 * p) for p in range(1, len(sends))]
    per = sends[0].shape[0] // 2
    own = jnp.concatenate([piece[:per] for piece in pieces], axis=0)
    partner = jnp.concatenate([piece[per:] for piece in pieces], axis=0)
    return [own, exchange(partner, "row", 1)]


def layer(
    node_feat, weight, bias, cotangent, blocks, row_block, col_block, live_blocks, send_list
):
    nodes, width = node_feat.shape
    groups, members = lax.axis_size("rep"), lax.axis_size("row")
    capacity = blocks.shape[2]
    per = send_list.shape[-1] // (members * members)
    slots = members * per
    row_blocks = groups * nodes // BS
    col_blocks = slots // BS
    rows = row_blocks * BS
    assert 2 * per == BS and nodes % BS == 0
    pairs = members // 2
    shape = lambda n: jax.ShapeDtypeStruct((n, width), F32)
    vmem = lambda n: pltpu.VMEM((n, width), F32)

    *sends, wanted = call(
        gather_rows,
        [shape(2 * per)] * pairs + [jax.ShapeDtypeStruct((1, slots), jnp.int32)],
        [pltpu.with_memory_space_constraint(x, pltpu.HBM) for x in (send_list, node_feat)],
        [vmem(nodes), vmem(slots), pltpu.SemaphoreType.DMA((2,))],
        hbm=(0, 1),
    )
    border = swap_rows(sends)
    wide = jax.ShapeDtypeStruct((rows, slots), BF16)
    tall = jax.ShapeDtypeStruct((slots, rows), BF16)
    bias_row = jax.ShapeDtypeStruct((1, width), F32)
    half_weight = jax.ShapeDtypeStruct(weight.shape, BF16)
    *dense, bias_here, weight_high, weight_low = call(
        functools.partial(build, nodes // BS),
        [wide, wide, tall, tall, bias_row, half_weight, half_weight],
        [live_blocks, row_block[0], col_block[0], blocks[0, 0], bias[None, :], weight],
        [pltpu.VMEM((slots // LANES, rows, LANES), F32)],
        flops=4 * row_blocks * col_blocks * capacity * BS * BS,
        smem=(0,),
    )
    partials = call(
        functools.partial(aggregate, pairs),
        [shape(nodes)] * groups,
        dense[:2] + border,
        flops=6 * rows * slots * width,
    )
    parts = [partials[0]] + [exchange(partials[s], "rep", s) for s in range(1, groups)]
    chunk = width // members
    padded = pairs * (chunk + PAD)
    pre, grad, keep, send = call(
        functools.partial(activate, groups, members),
        [shape(nodes), shape(nodes), shape(padded), shape(padded)],
        parts + [weight_high, weight_low, bias_here, cotangent],
        [vmem(width)],
        flops=12 * nodes * width * width,
    )
    (activated,) = call(emit, [shape(nodes)], [pre])
    grads = [grad] + [exchange(grad, "rep", s) for s in range(1, groups)]
    backs = call(
        functools.partial(spread, groups),
        [shape(2 * per)] * pairs,
        dense[2:] + grads,
        flops=6 * rows * slots * width,
    )
    returned = swap_rows(backs)
    (feat_grad,) = call(
        functools.partial(collect, per),
        [shape(nodes)],
        [wanted, weight_high, weight_low] + returned,
        [vmem(slots)],
        flops=6 * nodes * width * width,
    )
    total = keep + exchange(send, "row", 1)
    size = chunk + PAD
    owned = [total[p * size : (p + 1) * size] for p in range(pairs)]
    owned[1:] = [exchange(owned[p], "row", 2 * p) for p in range(1, pairs)]
    part = tree_sum(owned)
    summed = tree_sum([part] + [exchange(part, "rep", s) for s in range(1, groups)])
    done = summed[:chunk]
    chunks = [done] + [exchange(done, "row", 2 * p) for p in range(1, pairs)]
    own = jnp.concatenate(chunks, axis=0)
    partner = exchange(own, "row", 1)
    weight_grad, bias_grad = call(
        functools.partial(finish, members),
        [shape(width), shape(1)],
        [summed, own, partner],
    )
    return (activated, feat_grad, weight_grad, bias_grad[0])


def build(shard_blocks, live_ref, rows_ref, cols_ref, blocks_ref, bias_ref, weight_ref, *refs):
    high_ref, low_ref, high_t_ref, low_t_ref, bias_out, weight_high, weight_low, dense = refs
    bias_out[...] = bias_ref[...]
    weight_high[...], weight_low[...] = split(weight_ref[...])
    row_blocks = high_ref.shape[0] // BS
    col_blocks = high_ref.shape[1] // BS
    capacity = blocks_ref.shape[0]
    pairs = row_blocks * col_blocks
    me, group = lax.axis_index("row"), lax.axis_index("rep")
    rows = lax.bitwise_xor(rows_ref[...], group * shard_blocks)
    cols = lax.bitwise_xor(cols_ref[...], me // 2)
    pair = lax.broadcasted_iota(jnp.int32, (pairs, capacity), 0)
    slot = lax.broadcasted_iota(jnp.int32, (pairs, capacity), 1)
    pick = ((pair == cols * row_blocks + rows) & (slot < live_ref[0, 0])).astype(BF16)
    high, low = split(blocks_ref[...])
    product = mm(pick, high, NN) + mm(pick, low, NN)
    lane = lax.broadcasted_iota(jnp.int32, (row_blocks, LANES), 1)
    left = lane < BS
    upper = lane % BS < BS // 2
    same = me % 2 == 0
    for t in range(blocks_ref.shape[1] // LANES):
        lanes = slice(t * LANES, (t + 1) * LANES)
        for u in range(col_blocks // 2):
            first = product[2 * u * row_blocks : (2 * u + 1) * row_blocks, lanes]
            second = product[(2 * u + 1) * row_blocks : (2 * u + 2) * row_blocks, lanes]
            even = jnp.where(left, first, pltpu.roll(second, BS, 1))
            odd = jnp.where(left, pltpu.roll(first, BS, 1), second)
            for parity, value in ((0, even), (1, odd)):
                swapped = jnp.where(
                    upper, pltpu.roll(value, LANES - BS // 2, 1), pltpu.roll(value, BS // 2, 1)
                )
                value = jnp.where(same, value, swapped)
                dense[u, pl.ds(2 * t + parity, row_blocks, stride=BS), :] = value
    full = jnp.concatenate([dense[u] for u in range(col_blocks // 2)], axis=1)
    high_ref[...], low_ref[...] = split(full)
    high_t_ref[...], low_t_ref[...] = split(full.T)


def solution(mesh):
    return sharded(mesh)


def sharded(mesh):
    return jax.shard_map(
        layer,
        mesh=mesh,
        in_specs=(
            P(("rep", "row"), None),
            P(),
            P(),
            P(("rep", "row"), None),
            P("rep", "row", None, None),
            P("rep", "row", None),
            P("rep", "row", None),
            P("rep", "row"),
            P("rep", None),
        ),
        out_specs=(P(("rep", "row"), None), P(("rep", "row"), None), P(), P()),
        check_vma=False,
    )
```

```python
import functools

import jax
import jax.numpy as jnp
from jax import lax
from jax.experimental import pallas as pl
from jax.experimental.pallas import tpu as pltpu
from jax.sharding import PartitionSpec as P


BS = 64
LANES = 128
PAD = 8
FLOOR = 16 * 2**20
F32 = jnp.float32
BF16 = jnp.bfloat16
NN = (((1,), (0,)), ((), ()))
TN = (((0,), (0,)), ((), ()))
NT = (((1,), (1,)), ((), ()))


def split(x):
    high = x.astype(BF16)
    return high, (x - high.astype(F32)).astype(BF16)


def mm(a, b, dims):
    return lax.dot_general(a, b, dims, preferred_element_type=F32)


def mm3(a, b, dims):
    return mm(a[0], b[0], dims) + (mm(a[0], b[1], dims) + mm(a[1], b[0], dims))


def call(kernel, outs, args, scratch=(), flops=0, smem=(), hbm=()):
    out_bytes = sum(int(o.size) * o.dtype.itemsize for o in outs)
    in_bytes = sum(int(a.size) * a.dtype.itemsize for a in args)
    limit = max(FLOOR, 4 * (in_bytes + out_bytes))
    return pl.pallas_call(
        kernel,
        out_shape=outs,
        in_specs=[
            pl.BlockSpec(
                memory_space=pltpu.SMEM if k in smem else pltpu.HBM if k in hbm else pltpu.VMEM
            )
            for k in range(len(args))
        ],
        out_specs=[pl.BlockSpec(memory_space=pltpu.VMEM) for _ in outs],
        scratch_shapes=list(scratch),
        cost_estimate=pl.CostEstimate(
            flops=flops, transcendentals=0, bytes_accessed=in_bytes + out_bytes
        ),
        compiler_params=pltpu.CompilerParams(vmem_limit_bytes=limit),
    )(*args)


def rows_at(index, count):
    return pl.ds(pl.multiple_of(index * count, count), count)


def one_hot(wanted, nodes):
    node = lax.broadcasted_iota(jnp.int32, (nodes, wanted.shape[1]), 0)
    return (node == wanted).astype(BF16)


def tree_sum(terms):
    terms = list(terms)
    while len(terms) > 1:
        terms = [terms[k] + terms[k + 1] for k in range(0, len(terms), 2)]
    return terms[0]


def put_pairs(outs, buffer, me, per):
    for pair, out in enumerate(outs):
        for core in range(2):
            source = rows_at(lax.bitwise_xor(me, 2 * pair + core), per)
            out[core * per : (core + 1) * per, :] = buffer[source, :]


def take_pairs(own_ref, partner_ref, buffer, me, per):
    for pair in range(buffer.shape[0] // (2 * per)):
        rows = slice(pair * per, (pair + 1) * per)
        buffer[rows_at(lax.bitwise_xor(me, 2 * pair), per), :] = own_ref[rows, :]
        buffer[rows_at(lax.bitwise_xor(me, 2 * pair + 1), per), :] = partner_ref[rows, :]


def gather_rows(list_hbm, feat_hbm, *refs):
    outs, wanted_ref, feat_ref, buffer, sems = refs[:-4], refs[-4], refs[-3], refs[-2], refs[-1]
    me = lax.axis_index("row")
    slots = buffer.shape[0]
    copies = [
        pltpu.make_async_copy(feat_hbm, feat_ref, sems.at[0]),
        pltpu.make_async_copy(list_hbm.at[:, rows_at(me, slots)], wanted_ref, sems.at[1]),
    ]
    for copy in copies:
        copy.start()
    copies[1].wait()
    pick = one_hot(wanted_ref[...], feat_ref.shape[0]).T
    copies[0].wait()
    high, low = split(feat_ref[...])
    buffer[...] = mm(pick, high, NN) + mm(pick, low, NN)
    put_pairs(outs, buffer, me, outs[0].shape[0] // 2)


def aggregate(pairs, high_ref, low_ref, own_ref, partner_ref, *outs):
    per = own_ref.shape[0] // pairs
    same = lax.axis_index("row") % 2 == 0
    own, partner = own_ref[...], partner_ref[...]
    lower, upper = jnp.where(same, own, partner), jnp.where(same, partner, own)
    pieces = []
    for pair in range(pairs):
        for half in (lower, upper):
            pieces.append(half[pair * per : (pair + 1) * per, :])
    border = jnp.concatenate(pieces, axis=0)
    result = mm3((high_ref[...], low_ref[...]), split(border), NN)
    for s, out in enumerate(outs):
        out[...] = result[s * out.shape[0] : (s + 1) * out.shape[0], :]


def activate(groups, members, *refs):
    pieces = refs[:groups]
    high_ref, low_ref, bias_ref, cot_ref, pre_ref, grad_ref, keep_ref, send_ref, buffer = refs[groups:]
    me = lax.axis_index("row")
    total = tree_sum([piece[...] for piece in pieces])
    total_split = split(total)
    pre = mm3(total_split, (high_ref[...], low_ref[...]), NN) + bias_ref[...]
    gate = jax.nn.sigmoid(pre)
    pre_ref[...] = pre
    grad = cot_ref[...] * (gate * (1.0 + pre * (1.0 - gate)))
    grad_ref[...] = grad
    buffer[...] = mm3(total_split, split(grad), TN)
    chunk = buffer.shape[0] // members
    sums = jnp.broadcast_to(jnp.sum(grad, axis=0, keepdims=True), (PAD, grad.shape[1]))
    for s in range(members):
        target = send_ref if s % 2 else keep_ref
        start = (s // 2) * (chunk + PAD)
        target[start : start + chunk, :] = buffer[rows_at(lax.bitwise_xor(me, s), chunk), :]
        target[start + chunk : start + chunk + PAD, :] = sums


def spread(groups, high_ref, low_ref, *refs):
    pieces, outs = refs[:groups], refs[groups:]
    grads = jnp.concatenate([piece[...] for piece in pieces], axis=0)
    result = mm3((high_ref[...], low_ref[...]), split(grads), NN)
    same = lax.axis_index("row") % 2 == 0
    per = outs[0].shape[0] // 2
    for pair, out in enumerate(outs):
        lower = result[2 * pair * per : (2 * pair + 1) * per, :]
        upper = result[(2 * pair + 1) * per : (2 * pair + 2) * per, :]
        out[0:per, :] = jnp.where(same, lower, upper)
        out[per : 2 * per, :] = jnp.where(same, upper, lower)


def collect(per, wanted_ref, high_ref, low_ref, own_ref, partner_ref, out_ref, border):
    me = lax.axis_index("row")
    take_pairs(own_ref, partner_ref, border, me, per)
    pick = one_hot(wanted_ref[...], out_ref.shape[0])
    high, low = split(border[...])
    proj = mm(pick, high, NN) + mm(pick, low, NN)
    out_ref[...] = mm3(split(proj), (high_ref[...], low_ref[...]), NT)


def finish(members, summed_ref, own_ref, partner_ref, weight_ref, bias_ref):
    me = lax.axis_index("row")
    chunk = weight_ref.shape[0] // members
    for s in range(members):
        piece = partner_ref if s % 2 else own_ref
        start = (s // 2) * chunk
        weight_ref[rows_at(lax.bitwise_xor(me, s), chunk), :] = piece[start : start + chunk, :]
    bias_ref[...] = summed_ref[chunk : chunk + 1, :]


def emit(pre_ref, act_ref):
    pre = pre_ref[...]
    act_ref[...] = pre * jax.nn.sigmoid(pre)


def exchange(value, axis, shift):
    size = lax.axis_size(axis)
    return lax.ppermute(value, axis, [(i, i ^ shift) for i in range(size)])


def swap_rows(sends):
    pieces = [sends[0]]
    pieces += [exchange(sends[p], "row", 2 * p) for p in range(1, len(sends))]
    per = sends[0].shape[0] // 2
    own = jnp.concatenate([piece[:per] for piece in pieces], axis=0)
    partner = jnp.concatenate([piece[per:] for piece in pieces], axis=0)
    return [own, exchange(partner, "row", 1)]


def layer(
    node_feat, weight, bias, cotangent, blocks, row_block, col_block, live_blocks, send_list
):
    nodes, width = node_feat.shape
    groups, members = lax.axis_size("rep"), lax.axis_size("row")
    capacity = blocks.shape[2]
    per = send_list.shape[-1] // (members * members)
    slots = members * per
    row_blocks = groups * nodes // BS
    col_blocks = slots // BS
    rows = row_blocks * BS
    assert 2 * per == BS and nodes % BS == 0
    pairs = members // 2
    shape = lambda n: jax.ShapeDtypeStruct((n, width), F32)
    vmem = lambda n: pltpu.VMEM((n, width), F32)

    *sends, wanted = call(
        gather_rows,
        [shape(2 * per)] * pairs + [jax.ShapeDtypeStruct((1, slots), jnp.int32)],
        [pltpu.with_memory_space_constraint(x, pltpu.HBM) for x in (send_list, node_feat)],
        [vmem(nodes), vmem(slots), pltpu.SemaphoreType.DMA((2,))],
        hbm=(0, 1),
    )
    border = swap_rows(sends)
    wide = jax.ShapeDtypeStruct((rows, slots), BF16)
    tall = jax.ShapeDtypeStruct((slots, rows), BF16)
    bias_row = jax.ShapeDtypeStruct((1, width), F32)
    dense = call(
        functools.partial(build, nodes // BS),
        [wide, wide],
        [
            live_blocks,
            *(
                pltpu.with_memory_space_constraint(x, pltpu.HBM)
                for x in (row_block[0], col_block[0], blocks[0, 0])
            ),
        ],
        [
            pltpu.VMEM((1, capacity), jnp.int32),
            pltpu.VMEM((1, capacity), jnp.int32),
            pltpu.VMEM((capacity, BS * BS), F32),
            pltpu.VMEM((slots // LANES, rows, LANES), F32),
            pltpu.SemaphoreType.DMA((3,)),
        ],
        flops=4 * row_blocks * col_blocks * capacity * BS * BS,
        hbm=(1, 2, 3),
    )
    partials = call(
        functools.partial(aggregate, pairs),
        [shape(nodes)] * groups,
        [*dense, *border],
        flops=6 * rows * slots * width,
    )
    half_weight = jax.ShapeDtypeStruct(weight.shape, BF16)
    *turned, bias_here, weight_high, weight_low = call(
        prepare, [tall, tall, bias_row, half_weight, half_weight], [*dense, bias[None, :], weight]
    )
    parts = [partials[0]] + [exchange(partials[s], "rep", s) for s in range(1, groups)]
    chunk = width // members
    padded = pairs * (chunk + PAD)
    pre, grad, keep, send = call(
        functools.partial(activate, groups, members),
        [shape(nodes), shape(nodes), shape(padded), shape(padded)],
        parts + [weight_high, weight_low, bias_here, cotangent],
        [vmem(width)],
        flops=12 * nodes * width * width,
    )
    (activated,) = call(emit, [shape(nodes)], [pre])
    grads = [grad] + [exchange(grad, "rep", s) for s in range(1, groups)]
    backs = call(
        functools.partial(spread, groups),
        [shape(2 * per)] * pairs,
        turned + grads,
        flops=6 * rows * slots * width,
    )
    returned = swap_rows(backs)
    (feat_grad,) = call(
        functools.partial(collect, per),
        [shape(nodes)],
        [wanted, weight_high, weight_low] + returned,
        [vmem(slots)],
        flops=6 * nodes * width * width,
    )
    total = keep + exchange(send, "row", 1)
    size = chunk + PAD
    owned = [total[p * size : (p + 1) * size] for p in range(pairs)]
    owned[1:] = [exchange(owned[p], "row", 2 * p) for p in range(1, pairs)]
    part = tree_sum(owned)
    summed = tree_sum([part] + [exchange(part, "rep", s) for s in range(1, groups)])
    done = summed[:chunk]
    chunks = [done] + [exchange(done, "row", 2 * p) for p in range(1, pairs)]
    own = jnp.concatenate(chunks, axis=0)
    partner = exchange(own, "row", 1)
    weight_grad, bias_grad = call(
        functools.partial(finish, members),
        [shape(width), shape(1)],
        [summed, own, partner],
    )
    return (activated, feat_grad, weight_grad, bias_grad[0])


def build(shard_blocks, live_ref, rows_hbm, cols_hbm, blocks_hbm, high_ref, low_ref, *refs):
    rows_ref, cols_ref, blocks_ref, dense, sems = refs
    copies = [
        pltpu.make_async_copy(blocks_hbm, blocks_ref, sems.at[0]),
        pltpu.make_async_copy(rows_hbm, rows_ref, sems.at[1]),
        pltpu.make_async_copy(cols_hbm, cols_ref, sems.at[2]),
    ]
    for copy in copies:
        copy.start()
    for copy in copies[1:]:
        copy.wait()
    row_blocks = high_ref.shape[0] // BS
    col_blocks = high_ref.shape[1] // BS
    capacity = blocks_ref.shape[0]
    pairs = row_blocks * col_blocks
    me, group = lax.axis_index("row"), lax.axis_index("rep")
    rows = lax.bitwise_xor(rows_ref[...], group * shard_blocks)
    cols = lax.bitwise_xor(cols_ref[...], me // 2)
    pair = lax.broadcasted_iota(jnp.int32, (pairs, capacity), 0)
    slot = lax.broadcasted_iota(jnp.int32, (pairs, capacity), 1)
    pick = ((pair == cols * row_blocks + rows) & (slot < live_ref[...])).astype(BF16)
    copies[0].wait()
    high, low = split(blocks_ref[...])
    product = mm(pick, high, NN) + mm(pick, low, NN)
    left = lax.broadcasted_iota(jnp.int32, (row_blocks, LANES), 1) < BS
    for t in range(blocks_ref.shape[1] // LANES):
        lanes = slice(t * LANES, (t + 1) * LANES)
        for u in range(col_blocks // 2):
            first = product[2 * u * row_blocks : (2 * u + 1) * row_blocks, lanes]
            second = product[(2 * u + 1) * row_blocks : (2 * u + 2) * row_blocks, lanes]
            even = jnp.where(left, first, pltpu.roll(second, BS, 1))
            odd = jnp.where(left, pltpu.roll(first, BS, 1), second)
            for parity, value in ((0, even), (1, odd)):
                dense[u, pl.ds(2 * t + parity, row_blocks, stride=BS), :] = value
    for u in range(col_blocks // 2):
        lanes = slice(u * LANES, (u + 1) * LANES)
        high_ref[:, lanes], low_ref[:, lanes] = split(dense[u])


def prepare(high_ref, low_ref, bias_ref, weight_ref, *refs):
    high_t_ref, low_t_ref, bias_out, weight_high, weight_low = refs
    high_t_ref[...] = high_ref[...].astype(F32).T.astype(BF16)
    low_t_ref[...] = low_ref[...].astype(F32).T.astype(BF16)
    bias_out[...] = bias_ref[...]
    weight_high[...], weight_low[...] = split(weight_ref[...])


def solution(mesh):
    return sharded(mesh)


def sharded(mesh):
    return jax.shard_map(
        layer,
        mesh=mesh,
        in_specs=(
            P(("rep", "row"), None),
            P(),
            P(),
            P(("rep", "row"), None),
            P("rep", "row", None, None),
            P("rep", "row", None),
            P("rep", "row", None),
            P("rep", "row"),
            P("rep", None),
        ),
        out_specs=(P(("rep", "row"), None), P(("rep", "row"), None), P(), P()),
        check_vma=False,
    )
```

```python
import functools

import jax
import jax.numpy as jnp
from jax import lax
from jax.experimental import pallas as pl
from jax.experimental.pallas import tpu as pltpu
from jax.sharding import PartitionSpec as P


BS = 64
LANES = 128
PAD = 8
PARTS = 4
FLOOR = 16 * 2**20
F32 = jnp.float32
BF16 = jnp.bfloat16
NN = (((1,), (0,)), ((), ()))
TN = (((0,), (0,)), ((), ()))
NT = (((1,), (1,)), ((), ()))


def split(x):
    high = x.astype(BF16)
    return high, (x - high.astype(F32)).astype(BF16)


def mm(a, b, dims):
    return lax.dot_general(a, b, dims, preferred_element_type=F32)


def mm3(a, b, dims):
    return mm(a[0], b[0], dims) + (mm(a[0], b[1], dims) + mm(a[1], b[0], dims))


def call(kernel, outs, args, scratch=(), flops=0, smem=(), hbm=()):
    out_bytes = sum(int(o.size) * o.dtype.itemsize for o in outs)
    in_bytes = sum(int(a.size) * a.dtype.itemsize for a in args)
    limit = max(FLOOR, 4 * (in_bytes + out_bytes))
    return pl.pallas_call(
        kernel,
        out_shape=outs,
        in_specs=[
            pl.BlockSpec(
                memory_space=pltpu.SMEM if k in smem else pltpu.HBM if k in hbm else pltpu.VMEM
            )
            for k in range(len(args))
        ],
        out_specs=[pl.BlockSpec(memory_space=pltpu.VMEM) for _ in outs],
        scratch_shapes=list(scratch),
        cost_estimate=pl.CostEstimate(
            flops=flops, transcendentals=0, bytes_accessed=in_bytes + out_bytes
        ),
        compiler_params=pltpu.CompilerParams(vmem_limit_bytes=limit),
    )(*args)


def rows_at(index, count):
    return pl.ds(pl.multiple_of(index * count, count), count)


def one_hot(wanted, nodes):
    node = lax.broadcasted_iota(jnp.int32, (nodes, wanted.shape[1]), 0)
    return (node == wanted).astype(BF16)


def tree_sum(terms):
    terms = list(terms)
    while len(terms) > 1:
        terms = [terms[k] + terms[k + 1] for k in range(0, len(terms), 2)]
    return terms[0]


def put_pairs(outs, buffer, me, per):
    for pair, out in enumerate(outs):
        for core in range(2):
            source = rows_at(lax.bitwise_xor(me, 2 * pair + core), per)
            out[core * per : (core + 1) * per, :] = buffer[source, :]


def take_pairs(own_ref, partner_ref, buffer, me, per):
    for pair in range(buffer.shape[0] // (2 * per)):
        rows = slice(pair * per, (pair + 1) * per)
        buffer[rows_at(lax.bitwise_xor(me, 2 * pair), per), :] = own_ref[rows, :]
        buffer[rows_at(lax.bitwise_xor(me, 2 * pair + 1), per), :] = partner_ref[rows, :]


def copies_of(source, target, sems, first):
    rows = source.shape[0] // PARTS
    copies = []
    for k in range(PARTS):
        part = slice(k * rows, (k + 1) * rows)
        copies.append(
            pltpu.make_async_copy(source.at[part, :], target.at[part, :], sems.at[first + k])
        )
    return copies


def gather_rows(list_hbm, feat_hbm, *refs):
    outs, wanted_ref, feat_ref, buffer, sems = refs[:-4], refs[-4], refs[-3], refs[-2], refs[-1]
    me = lax.axis_index("row")
    slots = buffer.shape[0]
    wanted = pltpu.make_async_copy(list_hbm.at[:, rows_at(me, slots)], wanted_ref, sems.at[PARTS])
    copies = copies_of(feat_hbm, feat_ref, sems, 0)
    for copy in [wanted, *copies]:
        copy.start()
    wanted.wait()
    pick = one_hot(wanted_ref[...], feat_ref.shape[0]).T
    for copy in copies:
        copy.wait()
    high, low = split(feat_ref[...])
    buffer[...] = mm(pick, high, NN) + mm(pick, low, NN)
    put_pairs(outs, buffer, me, outs[0].shape[0] // 2)


def aggregate(pairs, high_ref, low_ref, own_ref, partner_ref, *outs):
    per = own_ref.shape[0] // pairs
    same = lax.axis_index("row") % 2 == 0
    own, partner = own_ref[...], partner_ref[...]
    lower, upper = jnp.where(same, own, partner), jnp.where(same, partner, own)
    pieces = []
    for pair in range(pairs):
        for half in (lower, upper):
            pieces.append(half[pair * per : (pair + 1) * per, :])
    border = jnp.concatenate(pieces, axis=0)
    result = mm3((high_ref[...], low_ref[...]), split(border), NN)
    for s, out in enumerate(outs):
        out[...] = result[s * out.shape[0] : (s + 1) * out.shape[0], :]


def activate(groups, members, *refs):
    pieces = refs[:groups]
    high_ref, low_ref, bias_ref, cot_ref, pre_ref, grad_ref, keep_ref, send_ref, buffer = refs[groups:]
    me = lax.axis_index("row")
    total = tree_sum([piece[...] for piece in pieces])
    total_split = split(total)
    pre = mm3(total_split, (high_ref[...], low_ref[...]), NN) + bias_ref[...]
    gate = jax.nn.sigmoid(pre)
    pre_ref[...] = pre
    grad = cot_ref[...] * (gate * (1.0 + pre * (1.0 - gate)))
    grad_ref[...] = grad
    buffer[...] = mm3(total_split, split(grad), TN)
    chunk = buffer.shape[0] // members
    sums = jnp.broadcast_to(jnp.sum(grad, axis=0, keepdims=True), (PAD, grad.shape[1]))
    for s in range(members):
        target = send_ref if s % 2 else keep_ref
        start = (s // 2) * (chunk + PAD)
        target[start : start + chunk, :] = buffer[rows_at(lax.bitwise_xor(me, s), chunk), :]
        target[start + chunk : start + chunk + PAD, :] = sums


def spread(groups, high_ref, low_ref, *refs):
    pieces, outs = refs[:groups], refs[groups:]
    grads = jnp.concatenate([piece[...] for piece in pieces], axis=0)
    result = mm3((high_ref[...], low_ref[...]), split(grads), NN)
    same = lax.axis_index("row") % 2 == 0
    per = outs[0].shape[0] // 2
    for pair, out in enumerate(outs):
        lower = result[2 * pair * per : (2 * pair + 1) * per, :]
        upper = result[(2 * pair + 1) * per : (2 * pair + 2) * per, :]
        out[0:per, :] = jnp.where(same, lower, upper)
        out[per : 2 * per, :] = jnp.where(same, upper, lower)


def collect(per, wanted_ref, high_ref, low_ref, own_ref, partner_ref, out_ref, border):
    me = lax.axis_index("row")
    take_pairs(own_ref, partner_ref, border, me, per)
    pick = one_hot(wanted_ref[...], out_ref.shape[0])
    high, low = split(border[...])
    proj = mm(pick, high, NN) + mm(pick, low, NN)
    out_ref[...] = mm3(split(proj), (high_ref[...], low_ref[...]), NT)


def finish(members, summed_ref, own_ref, partner_ref, weight_ref, bias_ref):
    me = lax.axis_index("row")
    chunk = weight_ref.shape[0] // members
    for s in range(members):
        piece = partner_ref if s % 2 else own_ref
        start = (s // 2) * chunk
        weight_ref[rows_at(lax.bitwise_xor(me, s), chunk), :] = piece[start : start + chunk, :]
    bias_ref[...] = summed_ref[chunk : chunk + 1, :]


def emit(pre_ref, act_ref):
    pre = pre_ref[...]
    act_ref[...] = pre * jax.nn.sigmoid(pre)


def exchange(value, axis, shift):
    size = lax.axis_size(axis)
    return lax.ppermute(value, axis, [(i, i ^ shift) for i in range(size)])


def swap_rows(sends):
    pieces = [sends[0]]
    pieces += [exchange(sends[p], "row", 2 * p) for p in range(1, len(sends))]
    per = sends[0].shape[0] // 2
    own = jnp.concatenate([piece[:per] for piece in pieces], axis=0)
    partner = jnp.concatenate([piece[per:] for piece in pieces], axis=0)
    return [own, exchange(partner, "row", 1)]


def layer(
    node_feat, weight, bias, cotangent, blocks, row_block, col_block, live_blocks, send_list
):
    nodes, width = node_feat.shape
    groups, members = lax.axis_size("rep"), lax.axis_size("row")
    capacity = blocks.shape[2]
    per = send_list.shape[-1] // (members * members)
    slots = members * per
    row_blocks = groups * nodes // BS
    col_blocks = slots // BS
    rows = row_blocks * BS
    assert 2 * per == BS and nodes % BS == 0
    pairs = members // 2
    shape = lambda n: jax.ShapeDtypeStruct((n, width), F32)
    vmem = lambda n: pltpu.VMEM((n, width), F32)

    *sends, wanted = call(
        gather_rows,
        [shape(2 * per)] * pairs + [jax.ShapeDtypeStruct((1, slots), jnp.int32)],
        [pltpu.with_memory_space_constraint(x, pltpu.HBM) for x in (send_list, node_feat)],
        [vmem(nodes), vmem(slots), pltpu.SemaphoreType.DMA((PARTS + 1,))],
        hbm=(0, 1),
    )
    border = swap_rows(sends)
    wide = jax.ShapeDtypeStruct((rows, slots), BF16)
    tall = jax.ShapeDtypeStruct((slots, rows), BF16)
    bias_row = jax.ShapeDtypeStruct((1, width), F32)
    dense = call(
        functools.partial(build, nodes // BS),
        [wide, wide],
        [
            live_blocks,
            *(
                pltpu.with_memory_space_constraint(x, pltpu.HBM)
                for x in (row_block[0], col_block[0], blocks[0, 0])
            ),
        ],
        [
            pltpu.VMEM((1, capacity), jnp.int32),
            pltpu.VMEM((1, capacity), jnp.int32),
            pltpu.VMEM((capacity, BS * BS), F32),
            pltpu.VMEM((slots // LANES, rows, LANES), F32),
            pltpu.SemaphoreType.DMA((PARTS + 2,)),
        ],
        flops=4 * row_blocks * col_blocks * capacity * BS * BS,
        hbm=(1, 2, 3),
    )
    partials = call(
        functools.partial(aggregate, pairs),
        [shape(nodes)] * groups,
        [*dense, *border],
        flops=6 * rows * slots * width,
    )
    half_weight = jax.ShapeDtypeStruct(weight.shape, BF16)
    *turned, bias_here, weight_high, weight_low = call(
        prepare, [tall, tall, bias_row, half_weight, half_weight], [*dense, bias[None, :], weight]
    )
    parts = [partials[0]] + [exchange(partials[s], "rep", s) for s in range(1, groups)]
    chunk = width // members
    padded = pairs * (chunk + PAD)
    pre, grad, keep, send = call(
        functools.partial(activate, groups, members),
        [shape(nodes), shape(nodes), shape(padded), shape(padded)],
        parts + [weight_high, weight_low, bias_here, cotangent],
        [vmem(width)],
        flops=12 * nodes * width * width,
    )
    (activated,) = call(emit, [shape(nodes)], [pre])
    grads = [grad] + [exchange(grad, "rep", s) for s in range(1, groups)]
    backs = call(
        functools.partial(spread, groups),
        [shape(2 * per)] * pairs,
        turned + grads,
        flops=6 * rows * slots * width,
    )
    returned = swap_rows(backs)
    (feat_grad,) = call(
        functools.partial(collect, per),
        [shape(nodes)],
        [wanted, weight_high, weight_low] + returned,
        [vmem(slots)],
        flops=6 * nodes * width * width,
    )
    total = keep + exchange(send, "row", 1)
    size = chunk + PAD
    owned = [total[p * size : (p + 1) * size] for p in range(pairs)]
    owned[1:] = [exchange(owned[p], "row", 2 * p) for p in range(1, pairs)]
    part = tree_sum(owned)
    summed = tree_sum([part] + [exchange(part, "rep", s) for s in range(1, groups)])
    done = summed[:chunk]
    chunks = [done] + [exchange(done, "row", 2 * p) for p in range(1, pairs)]
    own = jnp.concatenate(chunks, axis=0)
    partner = exchange(own, "row", 1)
    weight_grad, bias_grad = call(
        functools.partial(finish, members),
        [shape(width), shape(1)],
        [summed, own, partner],
    )
    return (activated, feat_grad, weight_grad, bias_grad[0])


def build(shard_blocks, live_ref, rows_hbm, cols_hbm, blocks_hbm, high_ref, low_ref, *refs):
    rows_ref, cols_ref, blocks_ref, dense, sems = refs
    places = [
        pltpu.make_async_copy(rows_hbm, rows_ref, sems.at[PARTS]),
        pltpu.make_async_copy(cols_hbm, cols_ref, sems.at[PARTS + 1]),
    ]
    copies = copies_of(blocks_hbm, blocks_ref, sems, 0)
    for copy in [*places, *copies]:
        copy.start()
    for copy in places:
        copy.wait()
    row_blocks = high_ref.shape[0] // BS
    col_blocks = high_ref.shape[1] // BS
    capacity = blocks_ref.shape[0]
    pairs = row_blocks * col_blocks
    me, group = lax.axis_index("row"), lax.axis_index("rep")
    rows = lax.bitwise_xor(rows_ref[...], group * shard_blocks)
    cols = lax.bitwise_xor(cols_ref[...], me // 2)
    pair = lax.broadcasted_iota(jnp.int32, (pairs, capacity), 0)
    slot = lax.broadcasted_iota(jnp.int32, (pairs, capacity), 1)
    pick = ((pair == cols * row_blocks + rows) & (slot < live_ref[...])).astype(BF16)
    for copy in copies:
        copy.wait()
    high, low = split(blocks_ref[...])
    product = mm(pick, high, NN) + mm(pick, low, NN)
    left = lax.broadcasted_iota(jnp.int32, (row_blocks, LANES), 1) < BS
    for t in range(blocks_ref.shape[1] // LANES):
        lanes = slice(t * LANES, (t + 1) * LANES)
        for u in range(col_blocks // 2):
            first = product[2 * u * row_blocks : (2 * u + 1) * row_blocks, lanes]
            second = product[(2 * u + 1) * row_blocks : (2 * u + 2) * row_blocks, lanes]
            even = jnp.where(left, first, pltpu.roll(second, BS, 1))
            odd = jnp.where(left, pltpu.roll(first, BS, 1), second)
            for parity, value in ((0, even), (1, odd)):
                dense[u, pl.ds(2 * t + parity, row_blocks, stride=BS), :] = value
    for u in range(col_blocks // 2):
        lanes = slice(u * LANES, (u + 1) * LANES)
        high_ref[:, lanes], low_ref[:, lanes] = split(dense[u])


def prepare(high_ref, low_ref, bias_ref, weight_ref, *refs):
    high_t_ref, low_t_ref, bias_out, weight_high, weight_low = refs
    high_t_ref[...] = high_ref[...].astype(F32).T.astype(BF16)
    low_t_ref[...] = low_ref[...].astype(F32).T.astype(BF16)
    bias_out[...] = bias_ref[...]
    weight_high[...], weight_low[...] = split(weight_ref[...])


def solution(mesh):
    return sharded(mesh)


def sharded(mesh):
    return jax.shard_map(
        layer,
        mesh=mesh,
        in_specs=(
            P(("rep", "row"), None),
            P(),
            P(),
            P(("rep", "row"), None),
            P("rep", "row", None, None),
            P("rep", "row", None),
            P("rep", "row", None),
            P("rep", "row"),
            P("rep", None),
        ),
        out_specs=(P(("rep", "row"), None), P(("rep", "row"), None), P(), P()),
        check_vma=False,
    )
```

```python
import functools

import jax
import jax.numpy as jnp
from jax import lax
from jax.experimental import pallas as pl
from jax.experimental.pallas import tpu as pltpu
from jax.sharding import PartitionSpec as P


BS = 64
LANES = 128
PAD = 8
PARTS = 4
FLOOR = 16 * 2**20
F32 = jnp.float32
BF16 = jnp.bfloat16
NN = (((1,), (0,)), ((), ()))
TN = (((0,), (0,)), ((), ()))
NT = (((1,), (1,)), ((), ()))


def split(x):
    high = x.astype(BF16)
    return high, (x - high.astype(F32)).astype(BF16)


def split3(x):
    high = x.astype(BF16)
    rest = x - high.astype(F32)
    middle = rest.astype(BF16)
    return high, middle, (rest - middle.astype(F32)).astype(BF16)


def mm(a, b, dims):
    return lax.dot_general(a, b, dims, preferred_element_type=F32)


def mm3(a, b, dims):
    return mm(a[0], b[0], dims) + (mm(a[0], b[1], dims) + mm(a[1], b[0], dims))


def mm6(a, b, dims):
    small = mm(a[0], b[2], dims) + mm(a[1], b[1], dims) + mm(a[2], b[0], dims)
    return mm(a[0], b[0], dims) + (mm(a[0], b[1], dims) + mm(a[1], b[0], dims) + small)


def selected(pick, x):
    high, middle, low = split3(x)
    return mm(pick, high, NN) + (mm(pick, middle, NN) + mm(pick, low, NN))


def call(kernel, outs, args, scratch=(), flops=0, smem=(), hbm=()):
    out_bytes = sum(int(o.size) * o.dtype.itemsize for o in outs)
    in_bytes = sum(int(a.size) * a.dtype.itemsize for a in args)
    limit = max(FLOOR, 4 * (in_bytes + out_bytes))
    return pl.pallas_call(
        kernel,
        out_shape=outs,
        in_specs=[
            pl.BlockSpec(
                memory_space=pltpu.SMEM if k in smem else pltpu.HBM if k in hbm else pltpu.VMEM
            )
            for k in range(len(args))
        ],
        out_specs=[pl.BlockSpec(memory_space=pltpu.VMEM) for _ in outs],
        scratch_shapes=list(scratch),
        cost_estimate=pl.CostEstimate(
            flops=flops, transcendentals=0, bytes_accessed=in_bytes + out_bytes
        ),
        compiler_params=pltpu.CompilerParams(vmem_limit_bytes=limit),
    )(*args)


def rows_at(index, count):
    return pl.ds(pl.multiple_of(index * count, count), count)


def one_hot(wanted, nodes):
    node = lax.broadcasted_iota(jnp.int32, (nodes, wanted.shape[1]), 0)
    return (node == wanted).astype(BF16)


def tree_sum(terms):
    terms = list(terms)
    while len(terms) > 1:
        terms = [terms[k] + terms[k + 1] for k in range(0, len(terms), 2)]
    return terms[0]


def put_pairs(outs, buffer, me, per):
    for pair, out in enumerate(outs):
        for core in range(2):
            source = rows_at(lax.bitwise_xor(me, 2 * pair + core), per)
            out[core * per : (core + 1) * per, :] = buffer[source, :]


def take_pairs(own_ref, partner_ref, buffer, me, per):
    for pair in range(buffer.shape[0] // (2 * per)):
        rows = slice(pair * per, (pair + 1) * per)
        buffer[rows_at(lax.bitwise_xor(me, 2 * pair), per), :] = own_ref[rows, :]
        buffer[rows_at(lax.bitwise_xor(me, 2 * pair + 1), per), :] = partner_ref[rows, :]


def copies_of(source, target, sems, first):
    rows = source.shape[0] // PARTS
    copies = []
    for k in range(PARTS):
        part = slice(k * rows, (k + 1) * rows)
        copies.append(
            pltpu.make_async_copy(source.at[part, :], target.at[part, :], sems.at[first + k])
        )
    return copies


def gather_rows(list_hbm, feat_hbm, *refs):
    outs, wanted_ref, feat_ref, buffer, sems = refs[:-4], refs[-4], refs[-3], refs[-2], refs[-1]
    me = lax.axis_index("row")
    slots = buffer.shape[0]
    wanted = pltpu.make_async_copy(list_hbm.at[:, rows_at(me, slots)], wanted_ref, sems.at[PARTS])
    copies = copies_of(feat_hbm, feat_ref, sems, 0)
    for copy in [wanted, *copies]:
        copy.start()
    wanted.wait()
    pick = one_hot(wanted_ref[...], feat_ref.shape[0]).T
    for copy in copies:
        copy.wait()
    buffer[...] = selected(pick, feat_ref[...])
    put_pairs(outs, buffer, me, outs[0].shape[0] // 2)


def aggregate(pairs, high_ref, middle_ref, low_ref, own_ref, partner_ref, *outs):
    per = own_ref.shape[0] // pairs
    same = lax.axis_index("row") % 2 == 0
    own, partner = own_ref[...], partner_ref[...]
    lower, upper = jnp.where(same, own, partner), jnp.where(same, partner, own)
    pieces = []
    for pair in range(pairs):
        for half in (lower, upper):
            pieces.append(half[pair * per : (pair + 1) * per, :])
    border = jnp.concatenate(pieces, axis=0)
    dense = high_ref[...], middle_ref[...], low_ref[...]
    result = mm6(dense, split3(border), NN)
    for s, out in enumerate(outs):
        out[...] = result[s * out.shape[0] : (s + 1) * out.shape[0], :]


def activate(groups, members, *refs):
    pieces = refs[:groups]
    high_ref, middle_ref, low_ref, bias_ref, cot_ref, pre_ref, grad_ref, keep_ref, send_ref, buffer = refs[groups:]
    me = lax.axis_index("row")
    total = tree_sum([piece[...] for piece in pieces])
    total_split = split3(total)
    weight = high_ref[...], middle_ref[...], low_ref[...]
    pre = mm6(total_split, weight, NN) + bias_ref[...]
    gate = jax.nn.sigmoid(pre)
    pre_ref[...] = pre
    grad = cot_ref[...] * (gate * (1.0 + pre * (1.0 - gate)))
    grad_ref[...] = grad
    buffer[...] = mm3(total_split, split(grad), TN)
    chunk = buffer.shape[0] // members
    sums = jnp.broadcast_to(jnp.sum(grad, axis=0, keepdims=True), (PAD, grad.shape[1]))
    for s in range(members):
        target = send_ref if s % 2 else keep_ref
        start = (s // 2) * (chunk + PAD)
        target[start : start + chunk, :] = buffer[rows_at(lax.bitwise_xor(me, s), chunk), :]
        target[start + chunk : start + chunk + PAD, :] = sums


def spread(groups, high_ref, low_ref, *refs):
    pieces, outs = refs[:groups], refs[groups:]
    grads = jnp.concatenate([piece[...] for piece in pieces], axis=0)
    result = mm3((high_ref[...], low_ref[...]), split(grads), NN)
    same = lax.axis_index("row") % 2 == 0
    per = outs[0].shape[0] // 2
    for pair, out in enumerate(outs):
        lower = result[2 * pair * per : (2 * pair + 1) * per, :]
        upper = result[(2 * pair + 1) * per : (2 * pair + 2) * per, :]
        out[0:per, :] = jnp.where(same, lower, upper)
        out[per : 2 * per, :] = jnp.where(same, upper, lower)


def collect(per, wanted_ref, high_ref, low_ref, own_ref, partner_ref, out_ref, border):
    me = lax.axis_index("row")
    take_pairs(own_ref, partner_ref, border, me, per)
    pick = one_hot(wanted_ref[...], out_ref.shape[0])
    high, low = split(border[...])
    proj = mm(pick, high, NN) + mm(pick, low, NN)
    out_ref[...] = mm3(split(proj), (high_ref[...], low_ref[...]), NT)


def finish(members, summed_ref, own_ref, partner_ref, weight_ref, bias_ref):
    me = lax.axis_index("row")
    chunk = weight_ref.shape[0] // members
    for s in range(members):
        piece = partner_ref if s % 2 else own_ref
        start = (s // 2) * chunk
        weight_ref[rows_at(lax.bitwise_xor(me, s), chunk), :] = piece[start : start + chunk, :]
    bias_ref[...] = summed_ref[chunk : chunk + 1, :]


def emit(pre_ref, act_ref):
    pre = pre_ref[...]
    act_ref[...] = pre * jax.nn.sigmoid(pre)


def exchange(value, axis, shift):
    size = lax.axis_size(axis)
    return lax.ppermute(value, axis, [(i, i ^ shift) for i in range(size)])


def swap_rows(sends):
    pieces = [sends[0]]
    pieces += [exchange(sends[p], "row", 2 * p) for p in range(1, len(sends))]
    per = sends[0].shape[0] // 2
    own = jnp.concatenate([piece[:per] for piece in pieces], axis=0)
    partner = jnp.concatenate([piece[per:] for piece in pieces], axis=0)
    return [own, exchange(partner, "row", 1)]


def layer(
    node_feat, weight, bias, cotangent, blocks, row_block, col_block, live_blocks, send_list
):
    nodes, width = node_feat.shape
    groups, members = lax.axis_size("rep"), lax.axis_size("row")
    capacity = blocks.shape[2]
    per = send_list.shape[-1] // (members * members)
    slots = members * per
    row_blocks = groups * nodes // BS
    col_blocks = slots // BS
    rows = row_blocks * BS
    assert 2 * per == BS and nodes % BS == 0
    pairs = members // 2
    shape = lambda n: jax.ShapeDtypeStruct((n, width), F32)
    vmem = lambda n: pltpu.VMEM((n, width), F32)

    *sends, wanted = call(
        gather_rows,
        [shape(2 * per)] * pairs + [jax.ShapeDtypeStruct((1, slots), jnp.int32)],
        [pltpu.with_memory_space_constraint(x, pltpu.HBM) for x in (send_list, node_feat)],
        [vmem(nodes), vmem(slots), pltpu.SemaphoreType.DMA((PARTS + 1,))],
        hbm=(0, 1),
    )
    border = swap_rows(sends)
    wide = jax.ShapeDtypeStruct((rows, slots), BF16)
    tall = jax.ShapeDtypeStruct((slots, rows), BF16)
    bias_row = jax.ShapeDtypeStruct((1, width), F32)
    dense = call(
        functools.partial(build, nodes // BS),
        [wide, wide, wide],
        [
            live_blocks,
            *(
                pltpu.with_memory_space_constraint(x, pltpu.HBM)
                for x in (row_block[0], col_block[0], blocks[0, 0])
            ),
        ],
        [
            pltpu.VMEM((1, capacity), jnp.int32),
            pltpu.VMEM((1, capacity), jnp.int32),
            pltpu.VMEM((capacity, BS * BS), F32),
            pltpu.VMEM((slots // LANES, rows, LANES), F32),
            pltpu.SemaphoreType.DMA((PARTS + 2,)),
        ],
        flops=4 * row_blocks * col_blocks * capacity * BS * BS,
        hbm=(1, 2, 3),
    )
    partials = call(
        functools.partial(aggregate, pairs),
        [shape(nodes)] * groups,
        [*dense, *border],
        flops=6 * rows * slots * width,
    )
    half_weight = jax.ShapeDtypeStruct(weight.shape, BF16)
    *turned, bias_here, weight_high, weight_middle, weight_low = call(
        prepare,
        [tall, tall, bias_row] + [half_weight] * 3,
        [*dense[:2], bias[None, :], weight],
    )
    parts = [partials[0]] + [exchange(partials[s], "rep", s) for s in range(1, groups)]
    chunk = width // members
    padded = pairs * (chunk + PAD)
    pre, grad, keep, send = call(
        functools.partial(activate, groups, members),
        [shape(nodes), shape(nodes), shape(padded), shape(padded)],
        parts + [weight_high, weight_middle, weight_low, bias_here, cotangent],
        [vmem(width)],
        flops=12 * nodes * width * width,
    )
    (activated,) = call(emit, [shape(nodes)], [pre])
    grads = [grad] + [exchange(grad, "rep", s) for s in range(1, groups)]
    backs = call(
        functools.partial(spread, groups),
        [shape(2 * per)] * pairs,
        turned + grads,
        flops=6 * rows * slots * width,
    )
    returned = swap_rows(backs)
    (feat_grad,) = call(
        functools.partial(collect, per),
        [shape(nodes)],
        [wanted, weight_high, weight_middle] + returned,
        [vmem(slots)],
        flops=6 * nodes * width * width,
    )
    total = keep + exchange(send, "row", 1)
    size = chunk + PAD
    owned = [total[p * size : (p + 1) * size] for p in range(pairs)]
    owned[1:] = [exchange(owned[p], "row", 2 * p) for p in range(1, pairs)]
    part = tree_sum(owned)
    summed = tree_sum([part] + [exchange(part, "rep", s) for s in range(1, groups)])
    done = summed[:chunk]
    chunks = [done] + [exchange(done, "row", 2 * p) for p in range(1, pairs)]
    own = jnp.concatenate(chunks, axis=0)
    partner = exchange(own, "row", 1)
    weight_grad, bias_grad = call(
        functools.partial(finish, members),
        [shape(width), shape(1)],
        [summed, own, partner],
    )
    return (activated, feat_grad, weight_grad, bias_grad[0])


def build(shard_blocks, live_ref, rows_hbm, cols_hbm, blocks_hbm, *refs):
    high_ref, middle_ref, low_ref, rows_ref, cols_ref, blocks_ref, dense, sems = refs
    places = [
        pltpu.make_async_copy(rows_hbm, rows_ref, sems.at[PARTS]),
        pltpu.make_async_copy(cols_hbm, cols_ref, sems.at[PARTS + 1]),
    ]
    copies = copies_of(blocks_hbm, blocks_ref, sems, 0)
    for copy in [*places, *copies]:
        copy.start()
    for copy in places:
        copy.wait()
    row_blocks = high_ref.shape[0] // BS
    col_blocks = high_ref.shape[1] // BS
    capacity = blocks_ref.shape[0]
    pairs = row_blocks * col_blocks
    me, group = lax.axis_index("row"), lax.axis_index("rep")
    rows = lax.bitwise_xor(rows_ref[...], group * shard_blocks)
    cols = lax.bitwise_xor(cols_ref[...], me // 2)
    pair = lax.broadcasted_iota(jnp.int32, (pairs, capacity), 0)
    slot = lax.broadcasted_iota(jnp.int32, (pairs, capacity), 1)
    pick = ((pair == cols * row_blocks + rows) & (slot < live_ref[...])).astype(BF16)
    for copy in copies:
        copy.wait()
    product = selected(pick, blocks_ref[...])
    left = lax.broadcasted_iota(jnp.int32, (row_blocks, LANES), 1) < BS
    for t in range(blocks_ref.shape[1] // LANES):
        lanes = slice(t * LANES, (t + 1) * LANES)
        for u in range(col_blocks // 2):
            first = product[2 * u * row_blocks : (2 * u + 1) * row_blocks, lanes]
            second = product[(2 * u + 1) * row_blocks : (2 * u + 2) * row_blocks, lanes]
            even = jnp.where(left, first, pltpu.roll(second, BS, 1))
            odd = jnp.where(left, pltpu.roll(first, BS, 1), second)
            for parity, value in ((0, even), (1, odd)):
                dense[u, pl.ds(2 * t + parity, row_blocks, stride=BS), :] = value
    for u in range(col_blocks // 2):
        lanes = slice(u * LANES, (u + 1) * LANES)
        high_ref[:, lanes], middle_ref[:, lanes], low_ref[:, lanes] = split3(dense[u])


def prepare(high_ref, low_ref, bias_ref, weight_ref, *refs):
    high_t_ref, low_t_ref, bias_out, weight_high, weight_middle, weight_low = refs
    high_t_ref[...] = high_ref[...].astype(F32).T.astype(BF16)
    low_t_ref[...] = low_ref[...].astype(F32).T.astype(BF16)
    bias_out[...] = bias_ref[...]
    weight_high[...], weight_middle[...], weight_low[...] = split3(weight_ref[...])


def solution(mesh):
    return sharded(mesh)


def sharded(mesh):
    return jax.shard_map(
        layer,
        mesh=mesh,
        in_specs=(
            P(("rep", "row"), None),
            P(),
            P(),
            P(("rep", "row"), None),
            P("rep", "row", None, None),
            P("rep", "row", None),
            P("rep", "row", None),
            P("rep", "row"),
            P("rep", None),
        ),
        out_specs=(P(("rep", "row"), None), P(("rep", "row"), None), P(), P()),
        check_vma=False,
    )
```

```python
import functools

import jax
import jax.numpy as jnp
from jax import lax
from jax.experimental import pallas as pl
from jax.experimental.pallas import tpu as pltpu
from jax.sharding import PartitionSpec as P


BS = 64
LANES = 128
PAD = 8
PARTS = 4
FLOOR = 16 * 2**20
F32 = jnp.float32
BF16 = jnp.bfloat16
NN = (((1,), (0,)), ((), ()))
TN = (((0,), (0,)), ((), ()))
NT = (((1,), (1,)), ((), ()))


def split(x):
    high = x.astype(BF16)
    return high, (x - high.astype(F32)).astype(BF16)


def split3(x):
    high = x.astype(BF16)
    rest = x - high.astype(F32)
    middle = rest.astype(BF16)
    return high, middle, (rest - middle.astype(F32)).astype(BF16)


def mm(a, b, dims):
    return lax.dot_general(a, b, dims, preferred_element_type=F32)


def mm3(a, b, dims):
    if dims == TN:
        return mm(a[0], b[0], dims) + (mm(a[0], b[1], dims) + mm(a[1], b[0], dims))
    rows = a[0].shape[0]
    first = mm(jnp.concatenate(a[:2], axis=0), b[0], dims)
    return first[:rows] + (mm(a[0], b[1], dims) + first[rows:])


def mm6(a, b):
    rows = a[0].shape[0]
    first = mm(jnp.concatenate(a, axis=0), b[0], NN)
    second = mm(jnp.concatenate(a[:2], axis=0), b[1], NN)
    small = mm(a[0], b[2], NN) + second[rows:] + first[2 * rows :]
    return first[:rows] + (second[:rows] + first[rows : 2 * rows] + small)


def selected(pick, x):
    high, middle, low = split3(x)
    return mm(pick, high, NN) + (mm(pick, middle, NN) + mm(pick, low, NN))


def call(kernel, outs, args, scratch=(), flops=0, smem=(), hbm=()):
    out_bytes = sum(int(o.size) * o.dtype.itemsize for o in outs)
    in_bytes = sum(int(a.size) * a.dtype.itemsize for a in args)
    limit = max(FLOOR, 4 * (in_bytes + out_bytes))
    return pl.pallas_call(
        kernel,
        out_shape=outs,
        in_specs=[
            pl.BlockSpec(
                memory_space=pltpu.SMEM if k in smem else pltpu.HBM if k in hbm else pltpu.VMEM
            )
            for k in range(len(args))
        ],
        out_specs=[pl.BlockSpec(memory_space=pltpu.VMEM) for _ in outs],
        scratch_shapes=list(scratch),
        cost_estimate=pl.CostEstimate(
            flops=flops, transcendentals=0, bytes_accessed=in_bytes + out_bytes
        ),
        compiler_params=pltpu.CompilerParams(vmem_limit_bytes=limit),
    )(*args)


def rows_at(index, count):
    return pl.ds(pl.multiple_of(index * count, count), count)


def one_hot(wanted, nodes):
    node = lax.broadcasted_iota(jnp.int32, (nodes, wanted.shape[1]), 0)
    return (node == wanted).astype(BF16)


def tree_sum(terms):
    terms = list(terms)
    while len(terms) > 1:
        terms = [terms[k] + terms[k + 1] for k in range(0, len(terms), 2)]
    return terms[0]


def put_pairs(outs, buffer, me, per):
    for pair, out in enumerate(outs):
        for core in range(2):
            source = rows_at(lax.bitwise_xor(me, 2 * pair + core), per)
            out[core * per : (core + 1) * per, :] = buffer[source, :]


def take_pairs(own_ref, partner_ref, buffer, me, per):
    for pair in range(buffer.shape[0] // (2 * per)):
        rows = slice(pair * per, (pair + 1) * per)
        buffer[rows_at(lax.bitwise_xor(me, 2 * pair), per), :] = own_ref[rows, :]
        buffer[rows_at(lax.bitwise_xor(me, 2 * pair + 1), per), :] = partner_ref[rows, :]


def copies_of(source, target, sems, first):
    rows = source.shape[0] // PARTS
    copies = []
    for k in range(PARTS):
        part = slice(k * rows, (k + 1) * rows)
        copies.append(
            pltpu.make_async_copy(source.at[part, :], target.at[part, :], sems.at[first + k])
        )
    return copies


def gather_rows(list_hbm, feat_hbm, *refs):
    outs, wanted_ref, feat_ref, buffer, sems = refs[:-4], refs[-4], refs[-3], refs[-2], refs[-1]
    me = lax.axis_index("row")
    slots = buffer.shape[0]
    wanted = pltpu.make_async_copy(list_hbm.at[:, rows_at(me, slots)], wanted_ref, sems.at[PARTS])
    copies = copies_of(feat_hbm, feat_ref, sems, 0)
    for copy in [wanted, *copies]:
        copy.start()
    wanted.wait()
    pick = one_hot(wanted_ref[...], feat_ref.shape[0]).T
    for copy in copies:
        copy.wait()
    buffer[...] = selected(pick, feat_ref[...])
    put_pairs(outs, buffer, me, outs[0].shape[0] // 2)


def aggregate(pairs, high_ref, middle_ref, low_ref, own_ref, partner_ref, *outs):
    per = own_ref.shape[0] // pairs
    same = lax.axis_index("row") % 2 == 0
    own, partner = own_ref[...], partner_ref[...]
    lower, upper = jnp.where(same, own, partner), jnp.where(same, partner, own)
    pieces = []
    for pair in range(pairs):
        for half in (lower, upper):
            pieces.append(half[pair * per : (pair + 1) * per, :])
    border = jnp.concatenate(pieces, axis=0)
    dense = high_ref[...], middle_ref[...], low_ref[...]
    result = mm6(dense, split3(border))
    for s, out in enumerate(outs):
        out[...] = result[s * out.shape[0] : (s + 1) * out.shape[0], :]


def activate(groups, members, *refs):
    pieces = refs[:groups]
    high_ref, middle_ref, low_ref, bias_ref, cot_ref, pre_ref, grad_ref, keep_ref, send_ref, buffer = refs[groups:]
    me = lax.axis_index("row")
    total = tree_sum([piece[...] for piece in pieces])
    total_split = split3(total)
    weight = high_ref[...], middle_ref[...], low_ref[...]
    pre = mm6(total_split, weight) + bias_ref[...]
    gate = jax.nn.sigmoid(pre)
    pre_ref[...] = pre
    grad = cot_ref[...] * (gate * (1.0 + pre * (1.0 - gate)))
    grad_ref[...] = grad
    buffer[...] = mm3(total_split, split(grad), TN)
    chunk = buffer.shape[0] // members
    sums = jnp.broadcast_to(jnp.sum(grad, axis=0, keepdims=True), (PAD, grad.shape[1]))
    for s in range(members):
        target = send_ref if s % 2 else keep_ref
        start = (s // 2) * (chunk + PAD)
        target[start : start + chunk, :] = buffer[rows_at(lax.bitwise_xor(me, s), chunk), :]
        target[start + chunk : start + chunk + PAD, :] = sums


def spread(groups, high_ref, low_ref, *refs):
    pieces, outs = refs[:groups], refs[groups:]
    grads = jnp.concatenate([piece[...] for piece in pieces], axis=0)
    result = mm3((high_ref[...], low_ref[...]), split(grads), NN)
    same = lax.axis_index("row") % 2 == 0
    per = outs[0].shape[0] // 2
    for pair, out in enumerate(outs):
        lower = result[2 * pair * per : (2 * pair + 1) * per, :]
        upper = result[(2 * pair + 1) * per : (2 * pair + 2) * per, :]
        out[0:per, :] = jnp.where(same, lower, upper)
        out[per : 2 * per, :] = jnp.where(same, upper, lower)


def collect(per, wanted_ref, high_ref, low_ref, own_ref, partner_ref, out_ref, border):
    me = lax.axis_index("row")
    take_pairs(own_ref, partner_ref, border, me, per)
    pick = one_hot(wanted_ref[...], out_ref.shape[0])
    high, low = split(border[...])
    proj = mm(pick, high, NN) + mm(pick, low, NN)
    out_ref[...] = mm3(split(proj), (high_ref[...], low_ref[...]), NT)


def finish(members, summed_ref, own_ref, partner_ref, weight_ref, bias_ref):
    me = lax.axis_index("row")
    chunk = weight_ref.shape[0] // members
    for s in range(members):
        piece = partner_ref if s % 2 else own_ref
        start = (s // 2) * chunk
        weight_ref[rows_at(lax.bitwise_xor(me, s), chunk), :] = piece[start : start + chunk, :]
    bias_ref[...] = summed_ref[chunk : chunk + 1, :]


def emit(pre_ref, act_ref):
    pre = pre_ref[...]
    act_ref[...] = pre * jax.nn.sigmoid(pre)


def exchange(value, axis, shift):
    size = lax.axis_size(axis)
    return lax.ppermute(value, axis, [(i, i ^ shift) for i in range(size)])


def swap_rows(sends):
    pieces = [sends[0]]
    pieces += [exchange(sends[p], "row", 2 * p) for p in range(1, len(sends))]
    per = sends[0].shape[0] // 2
    own = jnp.concatenate([piece[:per] for piece in pieces], axis=0)
    partner = jnp.concatenate([piece[per:] for piece in pieces], axis=0)
    return [own, exchange(partner, "row", 1)]


def layer(
    node_feat, weight, bias, cotangent, blocks, row_block, col_block, live_blocks, send_list
):
    nodes, width = node_feat.shape
    groups, members = lax.axis_size("rep"), lax.axis_size("row")
    capacity = blocks.shape[2]
    per = send_list.shape[-1] // (members * members)
    slots = members * per
    row_blocks = groups * nodes // BS
    col_blocks = slots // BS
    rows = row_blocks * BS
    assert 2 * per == BS and nodes % BS == 0
    pairs = members // 2
    shape = lambda n: jax.ShapeDtypeStruct((n, width), F32)
    vmem = lambda n: pltpu.VMEM((n, width), F32)

    *sends, wanted = call(
        gather_rows,
        [shape(2 * per)] * pairs + [jax.ShapeDtypeStruct((1, slots), jnp.int32)],
        [pltpu.with_memory_space_constraint(x, pltpu.HBM) for x in (send_list, node_feat)],
        [vmem(nodes), vmem(slots), pltpu.SemaphoreType.DMA((PARTS + 1,))],
        hbm=(0, 1),
    )
    border = swap_rows(sends)
    wide = jax.ShapeDtypeStruct((rows, slots), BF16)
    tall = jax.ShapeDtypeStruct((slots, rows), BF16)
    bias_row = jax.ShapeDtypeStruct((1, width), F32)
    dense = call(
        functools.partial(build, nodes // BS),
        [wide, wide, wide],
        [
            live_blocks,
            *(
                pltpu.with_memory_space_constraint(x, pltpu.HBM)
                for x in (row_block[0], col_block[0], blocks[0, 0])
            ),
        ],
        [
            pltpu.VMEM((1, capacity), jnp.int32),
            pltpu.VMEM((1, capacity), jnp.int32),
            pltpu.VMEM((capacity, BS * BS), F32),
            pltpu.VMEM((slots // LANES, rows, LANES), F32),
            pltpu.SemaphoreType.DMA((PARTS + 2,)),
        ],
        flops=4 * row_blocks * col_blocks * capacity * BS * BS,
        hbm=(1, 2, 3),
    )
    partials = call(
        functools.partial(aggregate, pairs),
        [shape(nodes)] * groups,
        [*dense, *border],
        flops=6 * rows * slots * width,
    )
    half_weight = jax.ShapeDtypeStruct(weight.shape, BF16)
    *turned, bias_here, weight_high, weight_middle, weight_low = call(
        prepare,
        [tall, tall, bias_row] + [half_weight] * 3,
        [*dense[:2], bias[None, :], weight],
    )
    parts = [partials[0]] + [exchange(partials[s], "rep", s) for s in range(1, groups)]
    chunk = width // members
    padded = pairs * (chunk + PAD)
    pre, grad, keep, send = call(
        functools.partial(activate, groups, members),
        [shape(nodes), shape(nodes), shape(padded), shape(padded)],
        parts + [weight_high, weight_middle, weight_low, bias_here, cotangent],
        [vmem(width)],
        flops=12 * nodes * width * width,
    )
    (activated,) = call(emit, [shape(nodes)], [pre])
    grads = [grad] + [exchange(grad, "rep", s) for s in range(1, groups)]
    backs = call(
        functools.partial(spread, groups),
        [shape(2 * per)] * pairs,
        turned + grads,
        flops=6 * rows * slots * width,
    )
    returned = swap_rows(backs)
    (feat_grad,) = call(
        functools.partial(collect, per),
        [shape(nodes)],
        [wanted, weight_high, weight_middle] + returned,
        [vmem(slots)],
        flops=6 * nodes * width * width,
    )
    total = keep + exchange(send, "row", 1)
    size = chunk + PAD
    owned = [total[p * size : (p + 1) * size] for p in range(pairs)]
    owned[1:] = [exchange(owned[p], "row", 2 * p) for p in range(1, pairs)]
    part = tree_sum(owned)
    summed = tree_sum([part] + [exchange(part, "rep", s) for s in range(1, groups)])
    done = summed[:chunk]
    chunks = [done] + [exchange(done, "row", 2 * p) for p in range(1, pairs)]
    own = jnp.concatenate(chunks, axis=0)
    partner = exchange(own, "row", 1)
    weight_grad, bias_grad = call(
        functools.partial(finish, members),
        [shape(width), shape(1)],
        [summed, own, partner],
    )
    return (activated, feat_grad, weight_grad, bias_grad[0])


def build(shard_blocks, live_ref, rows_hbm, cols_hbm, blocks_hbm, *refs):
    high_ref, middle_ref, low_ref, rows_ref, cols_ref, blocks_ref, dense, sems = refs
    places = [
        pltpu.make_async_copy(rows_hbm, rows_ref, sems.at[PARTS]),
        pltpu.make_async_copy(cols_hbm, cols_ref, sems.at[PARTS + 1]),
    ]
    copies = copies_of(blocks_hbm, blocks_ref, sems, 0)
    for copy in [*places, *copies]:
        copy.start()
    for copy in places:
        copy.wait()
    row_blocks = high_ref.shape[0] // BS
    col_blocks = high_ref.shape[1] // BS
    capacity = blocks_ref.shape[0]
    pairs = row_blocks * col_blocks
    me, group = lax.axis_index("row"), lax.axis_index("rep")
    rows = lax.bitwise_xor(rows_ref[...], group * shard_blocks)
    cols = lax.bitwise_xor(cols_ref[...], me // 2)
    pair = lax.broadcasted_iota(jnp.int32, (pairs, capacity), 0)
    slot = lax.broadcasted_iota(jnp.int32, (pairs, capacity), 1)
    pick = ((pair == cols * row_blocks + rows) & (slot < live_ref[...])).astype(BF16)
    for copy in copies:
        copy.wait()
    product = selected(pick, blocks_ref[...])
    left = lax.broadcasted_iota(jnp.int32, (row_blocks, LANES), 1) < BS
    for t in range(blocks_ref.shape[1] // LANES):
        lanes = slice(t * LANES, (t + 1) * LANES)
        for u in range(col_blocks // 2):
            first = product[2 * u * row_blocks : (2 * u + 1) * row_blocks, lanes]
            second = product[(2 * u + 1) * row_blocks : (2 * u + 2) * row_blocks, lanes]
            even = jnp.where(left, first, pltpu.roll(second, BS, 1))
            odd = jnp.where(left, pltpu.roll(first, BS, 1), second)
            for parity, value in ((0, even), (1, odd)):
                dense[u, pl.ds(2 * t + parity, row_blocks, stride=BS), :] = value
    for u in range(col_blocks // 2):
        lanes = slice(u * LANES, (u + 1) * LANES)
        high_ref[:, lanes], middle_ref[:, lanes], low_ref[:, lanes] = split3(dense[u])


def prepare(high_ref, low_ref, bias_ref, weight_ref, *refs):
    high_t_ref, low_t_ref, bias_out, weight_high, weight_middle, weight_low = refs
    high_t_ref[...] = high_ref[...].astype(F32).T.astype(BF16)
    low_t_ref[...] = low_ref[...].astype(F32).T.astype(BF16)
    bias_out[...] = bias_ref[...]
    weight_high[...], weight_middle[...], weight_low[...] = split3(weight_ref[...])


def solution(mesh):
    return sharded(mesh)


def sharded(mesh):
    return jax.shard_map(
        layer,
        mesh=mesh,
        in_specs=(
            P(("rep", "row"), None),
            P(),
            P(),
            P(("rep", "row"), None),
            P("rep", "row", None, None),
            P("rep", "row", None),
            P("rep", "row", None),
            P("rep", "row"),
            P("rep", None),
        ),
        out_specs=(P(("rep", "row"), None), P(("rep", "row"), None), P(), P()),
        check_vma=False,
    )
```
